512 devices in a mesh: seq: 128 (over z, y, core), fsdp: 4 (over x).
Axes of the slice: x: 4, y: 4, z: 16, core: 2. Of those that a mesh axis runs over, the one named last changes fastest.
Arguments:
- tokens: bfloat16 [4, 65536, 2048], P('fsdp', 'seq'), may hold values from -9 to 9
- qkv_weight: bfloat16 [2048, 1536], P('fsdp'), may hold values from -0.26516504 to 0.26516504
- near_offset: int32 [4], replicated, may hold values from 0 to 3
- far_offset: int32 [4], replicated, may hold values from 0 to 31
Outputs:
- mixed: bfloat16 [4, 65536, 512], P('fsdp', 'seq')
The draws below stay inside these ranges and needn't reach their ends.
All inputs are finite; a program needn't handle non-finite values.
Results may differ from the reference program's by a relative error of at most 0.0074.
Values may be sent and summed in bfloat16 or wider, within the bound.
A program may use at most 64 MiB of HBM per device.

```python
import jax
import jax.numpy as jnp
from jax import lax

D = 2048
HEADS = 4
HEAD_DIM = 128
BLOCK = 128
STRIDE = 8
TOK_DEV = 512
SEQS = 4
LEN = 65536
NEAR_RATE = 4
FAR_RATE = 32
N_SEQ = 128


def draw_tokens(key, part):
    random_part = jnp.clip(jax.random.normal(jax.random.fold_in(key, 1), (SEQS, LEN, D), jnp.float32), -6.0, 6.0)
    return random_part.astype(jnp.bfloat16)


def draw_qkv_weight(key, part):
    qkv_width = HEADS * HEAD_DIM
    column_scale = jnp.concatenate([jnp.full((qkv_width,), 1.6, jnp.float32), jnp.ones((2 * qkv_width,), jnp.float32)])
    drawn_part = jnp.clip(jax.random.normal(jax.random.fold_in(key, 5), (D, 3 * qkv_width), jnp.float32), -6.0, 6.0) * D ** (-0.5)
    drawn_part = drawn_part * column_scale[None, :]
    return drawn_part.astype(jnp.bfloat16)


def set_ends(values, own_key, least, high):
    longest = values.shape.index(max(values.shape))
    spots = []
    for shift in (0, 1):
        where = [jax.random.randint(jax.random.fold_in(own_key, axis), (), 0, length) for axis, length in enumerate(values.shape)]
        where[longest] = (where[longest] + shift) % values.shape[longest]
        spots.append(tuple(where))
    return values.at[spots[0]].set(least).at[spots[1]].set(high)


def setup_inputs(seed: int = 0) -> dict:
    key_of = jax.random.split(jax.random.key(seed), 5)
    return {
        "tokens": draw_tokens(jax.random.fold_in(key_of[4], 71), 0),
        "qkv_weight": draw_qkv_weight(jax.random.fold_in(key_of[4], 71), 0),
        "near_offset": set_ends(jax.random.randint(key_of[2], (HEADS,), 0, NEAR_RATE), jax.random.fold_in(key_of[2], 1), 0, NEAR_RATE - 1).astype(jnp.int32),
        "far_offset": set_ends(jax.random.randint(key_of[3], (HEADS,), 0, FAR_RATE), jax.random.fold_in(key_of[3], 1), 0, FAR_RATE - 1).astype(jnp.int32),
    }


NEG = -1e30


def causal_stats(packed):
    query, key_block, value_block = packed
    length_rows = query.shape[0]
    scores = jnp.einsum('qd,kd->qk', query.astype(jnp.float32), key_block.astype(jnp.float32)) * (HEAD_DIM ** -0.5)
    positions = jnp.arange(length_rows)
    scores = jnp.where(positions[None, :] <= positions[:, None], scores, NEG)
    best_score = jnp.max(scores, axis=1)
    weights = jnp.exp(scores - best_score[:, None])
    weight_sum = jnp.sum(weights, axis=1)
    rounded = lax.optimization_barrier(weights.astype(jnp.bfloat16))
    weighted = jnp.einsum('qk,kd->qd', rounded.astype(jnp.float32), value_block.astype(jnp.float32))
    return best_score, weight_sum, weighted


def reference(tokens, qkv_weight, near_offset, far_offset):
    def one_sequence(sequence):
        qkv_width = HEADS * HEAD_DIM
        device_count = N_SEQ
        block_rate = TOK_DEV // BLOCK
        near_size = min(16, N_SEQ)
        half_size = near_size // 2
        far_size = min(16, N_SEQ // STRIDE)
        far_groups = device_count // (STRIDE * far_size)
        head_index = jnp.arange(HEADS)
        projected = jnp.dot(sequence, qkv_weight, preferred_element_type=jnp.float32).astype(jnp.bfloat16)
        query = projected[:, :qkv_width].reshape(LEN, HEADS, HEAD_DIM)
        key_all = projected[:, qkv_width:2 * qkv_width].reshape(LEN, HEADS, HEAD_DIM)
        value_all = projected[:, 2 * qkv_width:].reshape(LEN, HEADS, HEAD_DIM)

        def local_view(field):
            arranged = field.reshape(device_count, TOK_DEV, HEADS, HEAD_DIM).transpose(0, 2, 1, 3)
            return arranged.reshape(device_count * HEADS, TOK_DEV, HEAD_DIM)

        local_top, local_sum, local_out = lax.map(causal_stats, (local_view(query), local_view(key_all), local_view(value_all)))
        local_top = local_top.reshape(device_count, HEADS, block_rate, BLOCK)
        local_sum = local_sum.reshape(device_count, HEADS, block_rate, BLOCK)
        local_out = local_out.reshape(device_count, HEADS, block_rate, BLOCK, HEAD_DIM)

        def near_view(field):
            blocks = field.reshape(device_count, block_rate, BLOCK, HEADS, HEAD_DIM)
            picked = blocks[:, near_offset, :, head_index, :]
            padding = jnp.zeros((HEADS, half_size, BLOCK, HEAD_DIM), picked.dtype)
            assembled = jnp.concatenate([picked[:, :half_size], padding, picked[:, half_size:], padding], axis=1)
            return assembled.reshape(HEADS * (device_count // near_size + 1), near_size * BLOCK, HEAD_DIM)

        def near_back(field):
            shaped = field.reshape((HEADS, device_count + near_size) + field.shape[1:][:0] + (BLOCK,) + field.shape[2:])
            return jnp.concatenate([shaped[:, :half_size], shaped[:, near_size:device_count + half_size]], axis=1)

        near_top, near_sum, near_out = lax.map(causal_stats, (near_view(query), near_view(key_all), near_view(value_all)))
        near_top = near_back(near_top.reshape(HEADS, (device_count + near_size) * BLOCK)).transpose(1, 0, 2)[:, :, None, :]
        near_sum = near_back(near_sum.reshape(HEADS, (device_count + near_size) * BLOCK)).transpose(1, 0, 2)[:, :, None, :]
        near_out = near_back(near_out.reshape(HEADS, (device_count + near_size) * BLOCK, HEAD_DIM)).transpose(1, 0, 2, 3)[:, :, None, :, :]
        near_mask = (jnp.arange(block_rate)[None, :] == near_offset[:, None])[None, :, :, None]
        near_top = jnp.where(near_mask, near_top, NEG)

        far_class = far_offset // block_rate
        far_block = far_offset % block_rate

        def far_view(field):
            blocks = field.reshape(far_groups, far_size, STRIDE, block_rate, BLOCK, HEADS, HEAD_DIM)
            picked = blocks[:, :, far_class, far_block, :, head_index, :]
            return picked.reshape(HEADS * far_groups, far_size * BLOCK, HEAD_DIM)

        far_top, far_sum, far_out = lax.map(causal_stats, (far_view(query), far_view(key_all), far_view(value_all)))
        full_shape = (far_groups, far_size, STRIDE, HEADS, block_rate, BLOCK)

        def spread(field):
            arranged = field.reshape(HEADS, far_groups, far_size, BLOCK).transpose(1, 2, 0, 3)[:, :, None, :, None, :]
            return jnp.broadcast_to(arranged, full_shape).reshape(device_count, HEADS, block_rate, BLOCK)

        far_top_full = spread(far_top)
        far_sum_full = spread(far_sum)
        arranged_out = far_out.reshape(HEADS, far_groups, far_size, BLOCK, HEAD_DIM).transpose(1, 2, 0, 3, 4)[:, :, None, :, None, :, :]
        far_out_full = jnp.broadcast_to(arranged_out, full_shape + (HEAD_DIM,)).reshape(device_count, HEADS, block_rate, BLOCK, HEAD_DIM)
        class_match = jnp.arange(STRIDE)[:, None, None] == far_class[None, :, None]
        block_match = jnp.arange(block_rate)[None, None, :] == far_block[None, :, None]
        far_mask = jnp.broadcast_to((class_match & block_match)[None, None, :, :, :, None], full_shape).reshape(device_count, HEADS, block_rate, BLOCK)
        far_top_full = jnp.where(far_mask, far_top_full, NEG)

        best_score = jnp.maximum(jnp.maximum(local_top, near_top), far_top_full)
        local_weight = jnp.exp(local_top - best_score)
        near_weight = jnp.where(near_mask, jnp.exp(near_top - best_score), 0.0)
        far_weight = jnp.where(far_mask, jnp.exp(far_top_full - best_score), 0.0)
        numerator = local_weight[..., None] * local_out + near_weight[..., None] * near_out + far_weight[..., None] * far_out_full
        denominator = local_weight * local_sum + near_weight * near_sum + far_weight * far_sum_full
        mixed = numerator / denominator[..., None]
        return mixed.transpose(0, 2, 3, 1, 4).reshape(LEN, qkv_width).astype(jnp.bfloat16)

    return lax.map(one_sequence, tokens)
```

```python
import jax
import jax.numpy as jnp
from jax import lax
from jax.experimental import pallas as pl
from jax.experimental.pallas import tpu as pltpu
from jax.sharding import PartitionSpec as P

HEADS = 4
HD = 128
NZ = 16
SCALE = HD ** (-0.5)
NEG = -1e30
BF = jnp.bfloat16
F32 = jnp.float32

X_DIR, X_FWD, Y_W, Z_W, C_W = 0, 4, 8, 11, 14
F_SIB, F_PLANE, N_Q, N_KV, N_SIB, N_UP, N_UPSIB = 26, 27, 30, 33, 36, 37, 38
R_UP, R_DN, N_O, N_L, F_O, F_L = 39, 47, 54, 57, 60, 67
N_SEM = 74


def qk(q, k):
    return lax.dot_general(q, k, (((1,), (1,)), ((), ())), preferred_element_type=F32) * SCALE


def pv(p, v):
    return jnp.dot(p.astype(BF), v, preferred_element_type=F32)


def lanes(column):
    return jnp.broadcast_to(column, (128, 128))


def kernel(tok, wgt, noff, foff, out, wfull, tokv, acc, proj, fa_snd, fa_rcv, fsel, fcand, kvf,
           nqs, nks, nq, nkv, ncross, nm, nl, no, nos, nls, nor, nlr, fos, fls, fo, fl, lo, ll,
           ssem, rsem, lsem):
    seq = lax.axis_index("seq")
    x = lax.axis_index("fsdp")
    z = lax.div(seq, 8)
    y = lax.rem(lax.div(seq, 2), 4)
    c = lax.rem(seq, 2)
    oc = 1 - c

    def dev(dx=0, dy=0, dz=0, core=c):
        return (lax.rem(z + dz, NZ) * 8 + lax.rem(y + dy, 4) * 2 + core, lax.rem(x + dx, 4))

    def rc(k, src, dst, to):
        return pltpu.make_async_remote_copy(
            src_ref=src, dst_ref=dst, send_sem=ssem.at[k], recv_sem=rsem.at[k],
            device_id=to, device_id_type=pl.DeviceIdType.MESH)

    loads = []
    for k in range(4):
        loads.append(pltpu.make_async_copy(tok.at[:, pl.ds(512 * k, 512)], tokv.at[k], lsem.at[k]))
        loads.append(pltpu.make_async_copy(wgt.at[:, pl.ds(384 * k, 384)], wfull.at[0, k], lsem.at[4 + k]))
    for ld in loads:
        ld.start()
    barrier = pltpu.get_barrier_semaphore()
    peers = [dev(dx=1), dev(dx=3), dev(dz=1), dev(dz=NZ - 1), dev(core=oc)]
    for dy in (1, 2, 3):
        peers += [dev(dy=dy), dev(dy=dy, core=oc)]
    for peer in peers:
        pl.semaphore_signal(barrier, inc=1, device_id=peer, device_id_type=pl.DeviceIdType.MESH)
    pl.semaphore_wait(barrier, len(peers))

    ya, za = lax.rem(y, 2), 2 + lax.rem(z, 2)
    aset = (ya, za)
    bset = (1 - ya, 5 - za)
    half = pl.ds(pl.multiple_of(256 * c, 256), 256)
    pend = []
    xd = {}
    for a in (0, 1):
        for slot, dx, k in ((3, 1, 0), (1, 3, 1)):
            src = wgt.at[half, pl.ds(pl.multiple_of(384 * aset[a], 128), 384)]
            cp = rc(X_DIR + 2 * a + k, src, wfull.at[slot, aset[a], half], dev(dx=dx))
            cp.start()
            xd[a, slot] = cp
            pend.append(cp)

    for ld in loads:
        ld.wait()

    def mm(slot, s, first=False):
        r = jnp.dot(tokv[lax.rem(x + slot, 4)], wfull[slot, s], preferred_element_type=F32)
        if first:
            acc[s] = r
        else:
            acc[s] += r

    for s in range(4):
        mm(0, s, True)

    cw, nb, xf = {}, {}, {}

    def core_send(role, slot, s):
        k = C_W + role * 3 + slot - 1
        cp = rc(k, wfull.at[slot, s, half], wfull.at[slot, s, half], dev(core=oc))
        cp.start()
        cw[role, slot] = cp
        pend.append(cp)

    step = 1 + 2 * c
    zstep = 1 + (NZ - 2) * c

    def side_send(a, slot):
        to = dev(dy=step) if a == 0 else dev(dz=zstep)
        k = (Y_W if a == 0 else Z_W) + slot - 1
        cp = rc(k, wfull.at[slot, aset[a], half], wfull.at[slot, aset[a], half], to)
        cp.start()
        nb[a, slot] = cp
        pend.append(cp)

    for a in (0, 1):
        for slot in (3, 1):
            xd[a, slot].wait_recv()
            row = 256 * c + (0 if slot == 3 else 128)
            part = pl.ds(pl.multiple_of(row, 128), 128)
            k = 0 if slot == 3 else 1
            cp = rc(X_FWD + 2 * a + k, wfull.at[slot, aset[a], part], wfull.at[2, aset[a], part],
                    dev(dx=1 if slot == 3 else 3))
            cp.start()
            xf[a, k] = cp
            pend.append(cp)
            side_send(a, slot)
            core_send(a, slot, aset[a])
    for a in (0, 1):
        for slot in (3, 1):
            cw[a, slot].wait_recv()
            mm(slot, aset[a])
    for slot in (3, 1):
        for a in (0, 1):
            nb[a, slot].wait_recv()
            core_send(2 + a, slot, bset[a])
    for a in (0, 1):
        xf[a, 0].wait_recv()
        xf[a, 1].wait_recv()
        side_send(a, 2)
        core_send(a, 2, aset[a])
    for slot in (3, 1):
        for a in (0, 1):
            cw[2 + a, slot].wait_recv()
            mm(slot, bset[a])
    for a in (0, 1):
        cw[a, 2].wait_recv()
        mm(2, aset[a])
    for a in (0, 1):
        nb[a, 2].wait_recv()
        core_send(2 + a, 2, bset[a])
    for a in (0, 1):
        cw[2 + a, 2].wait_recv()
        mm(2, bset[a])
    for j in range(12):
        proj[j] = acc[j // 3, :, (j % 3) * 128:(j % 3) * 128 + 128].astype(BF).reshape(8, 64, 128)

    def rows(j, b):
        return proj[j, pl.ds(2 * b, 2)].reshape(128, HD)

    def half_rows(j, b, which):
        return proj[j, 2 * b + which]

    def span(j, n, m):
        return proj[j, n // 64:m // 64].reshape(m - n, HD)

    fb = [lax.rem(foff[h], 4) for h in range(HEADS)]
    fc = [lax.div(foff[h], 4) for h in range(HEADS)]
    nbk = [noff[h] for h in range(HEADS)]
    for h in range(HEADS):
        fa_snd[h, 0:128] = rows(h, fb[h])
        fa_snd[h, 128:192] = half_rows(4 + h, fb[h], oc)
        fa_snd[h, 192:256] = half_rows(8 + h, fb[h], oc)
    fsib = rc(F_SIB, fa_snd, fa_rcv, dev(core=oc))
    fsib.start()
    pend.append(fsib)
    for h in range(HEADS):
        nqs[h] = rows(h, nbk[h])
        nks[h, 0] = rows(4 + h, nbk[h])
        nks[h, 1] = rows(8 + h, nbk[h])
    nin = []
    for j in (1, 2, 3):
        t = lax.rem(y + j, 4)
        for k, src, dst in ((N_Q, nqs.at[t], nq.at[y]), (N_KV, nks.at[t], nkv.at[c, :, y])):
            cp = rc(k + j - 1, src, dst, dev(dy=j))
            cp.start()
            nin.append(cp)
            pend.append(cp)
    nq[y] = nqs[y]
    nkv[c, 0, y] = nks[y, 0]
    nkv[c, 1, y] = nks[y, 1]

    qi = lax.broadcasted_iota(jnp.int32, (128, 128), 0)
    ki = lax.broadcasted_iota(jnp.int32, (128, 128), 1)
    causal = ki <= qi

    def local(h, i):
        n = 128 * i
        q = span(h, n, n + 128)
        s1 = jnp.where(causal, qk(q, span(4 + h, n, n + 128)), NEG)
        top = jnp.max(s1, axis=1, keepdims=True)
        if i:
            s0 = qk(q, span(4 + h, 0, n))
            top = jnp.maximum(top, jnp.max(s0, axis=1, keepdims=True))
        p1 = jnp.exp(s1 - top)
        tot = jnp.sum(p1, axis=1, keepdims=True)
        o = pv(p1, span(8 + h, n, n + 128))
        if i:
            p0 = jnp.exp(s0 - top)
            tot = tot + jnp.sum(p0, axis=1, keepdims=True)
            o = o + pv(p0, span(8 + h, 0, n))
        lo[h, i] = o / tot
        ll[h, i] = lanes(top + jnp.log(tot))

    for i in range(4):
        local(0, i)

    fsib.wait_recv()
    for h in range(HEADS):
        mine = jnp.full((128, HD), lax.rem(fc[h], 2), jnp.int32) == c

        def pick(own, other):
            return jnp.where(mine[0:own.shape[0]], own.astype(F32), other.astype(F32)).astype(BF)

        fsel[h, 0:128] = pick(rows(h, fb[h]), fa_rcv[h, 0:128])
        fsel[h, 128:192] = pick(half_rows(4 + h, fb[h], c), fa_rcv[h, 128:192])
        fsel[h, 192:256] = pick(half_rows(8 + h, fb[h], c), fa_rcv[h, 192:256])
    fin = []
    for j in (1, 2, 3):
        cp = rc(F_PLANE + j - 1, fsel.at[lax.rem(y + j, 4)], fcand.at[y], dev(dy=j))
        cp.start()
        fin.append(cp)
        pend.append(cp)
    fcand[y] = fsel[y]

    for cp in nin:
        cp.wait_recv()
    nsib = rc(N_SIB, nkv.at[c], nkv.at[c], dev(core=oc))
    nsib.start()
    pend.append(nsib)
    nup = rc(N_UP, nkv.at[c], ncross.at[c], dev(dz=1))
    odd = lax.rem(z, 2) == 1
    even = lax.rem(z, 2) == 0

    @pl.when(odd)
    def _():
        nup.start()

    for i in range(4):
        local(1, i)

    for cp in fin:
        cp.wait_recv()
    holder = lax.div(foff[y], 8)
    fq = fcand[holder, 0:128]
    kvf[0, 0] = fcand[holder, 128:192]
    kvf[0, 1] = fcand[holder, 192:256]

    ups, dns = {}, {}

    def send_up(t):
        ups[t] = rc(R_UP + t - 1, kvf.at[t - 1], kvf.at[t], dev(dz=1))
        ups[t].start()
        pend.append(ups[t])

    def send_dn(t):
        src = 0 if t == 1 else 17 - t
        dns[t] = rc(R_DN + t - 1, kvf.at[src], kvf.at[16 - t], dev(dz=NZ - 1))
        dns[t].start()
        pend.append(dns[t])

    send_up(1)
    send_dn(1)

    def ring(t):
        ups[t].wait_recv()
        if t < 8:
            send_up(t + 1)
        if t < 8:
            dns[t].wait_recv()
            if t < 7:
                send_dn(t + 1)

    for i in range(4):
        local(2, i)
    ring(1)
    for i in range(4):
        local(3, i)
    ring(2)

    nsib.wait_recv()

    def near_plane(i):
        q = nq[i]
        m = 128 * (i + 1)
        sa = qk(q, nkv[c, 0, 0:i + 1].reshape(m, HD))
        sb = qk(q, nkv[oc, 0, 0:i + 1].reshape(m, HD))
        kk = lax.broadcasted_iota(jnp.int32, (128, m), 1)
        qq = lax.broadcasted_iota(jnp.int32, (128, m), 0) + 128 * i
        sa = jnp.where(kk <= qq, sa, NEG)
        sb = jnp.where(kk < 128 * (i + c), sb, NEG)
        top = jnp.maximum(jnp.max(sa, axis=1, keepdims=True), jnp.max(sb, axis=1, keepdims=True))
        pa = jnp.exp(sa - top)
        pb = jnp.exp(sb - top)
        tot = jnp.sum(pa, axis=1, keepdims=True) + jnp.sum(pb, axis=1, keepdims=True)
        no[i] = pv(pa, nkv[c, 1, 0:i + 1].reshape(m, HD)) + pv(pb, nkv[oc, 1, 0:i + 1].reshape(m, HD))
        nm[i] = lanes(top)
        nl[i] = lanes(tot)

    nupsib = rc(N_UPSIB, ncross.at[c], ncross.at[c], dev(core=oc))

    @pl.when(even)
    def _():
        nup.wait_recv()
        nupsib.start()

    near_plane(0)
    near_plane(1)
    ring(3)
    near_plane(2)
    ring(4)
    near_plane(3)
    ring(5)

    @pl.when(even)
    def _():
        nupsib.wait_recv()

    def near_cross(i):
        q = nq[i]
        ss = [qk(q, ncross[d, 0].reshape(512, HD)) for d in (0, 1)]
        old = nm[i][:, 0:1]
        top = jnp.maximum(old, jnp.maximum(jnp.max(ss[0], axis=1, keepdims=True),
                                           jnp.max(ss[1], axis=1, keepdims=True)))
        w = jnp.exp(old - top)
        ps = [jnp.exp(s - top) for s in ss]
        tot = w * nl[i][:, 0:1] + jnp.sum(ps[0], axis=1, keepdims=True) + jnp.sum(ps[1], axis=1, keepdims=True)
        no[i] = w * no[i] + pv(ps[0], ncross[0, 1].reshape(512, HD)) + pv(ps[1], ncross[1, 1].reshape(512, HD))
        nm[i] = lanes(top)
        nl[i] = lanes(tot)

    cross = even & (z > 0)

    @pl.when(cross)
    def _():
        near_cross(0)
        near_cross(1)

    ring(6)

    @pl.when(cross)
    def _():
        near_cross(2)
        near_cross(3)

    ring(7)

    for i in range(4):
        nos[i] = (no[i] / nl[i]).astype(BF)
        nls[i] = (nm[i] + jnp.log(nl[i])).T[0:8]
    nback = []
    for j in (1, 2, 3):
        t = lax.rem(y + j, 4)
        for k, src, dst in ((N_O, nos.at[t], nor.at[y]), (N_L, nls.at[t], nlr.at[y])):
            cp = rc(k + j - 1, src, dst, dev(dy=j))
            cp.start()
            nback.append(cp)
            pend.append(cp)
    nor[y] = nos[y]
    nlr[y] = nls[y]

    ring(8)

    sf = qk(fq, kvf[:, 0].reshape(1024, HD))
    kk = lax.broadcasted_iota(jnp.int32, (128, 1024), 1)
    qq = lax.broadcasted_iota(jnp.int32, (128, 1024), 0)
    dist = lax.shift_right_logical(kk, 6)
    seen = (dist <= z) & ((dist > 0) | (kk + 64 * c <= qq))
    sf = jnp.where(seen, sf, NEG)
    top = jnp.max(sf, axis=1, keepdims=True)
    pf = jnp.exp(sf - top)
    tot = jnp.sum(pf, axis=1, keepdims=True)
    fos[...] = (pv(pf, kvf[:, 1].reshape(1024, HD)) / tot).astype(BF)
    fls[...] = lanes(top + jnp.log(tot)).T[0:8]
    fback = []
    n = 0
    for dy in (0, 1, 2, 3):
        for core in (c, oc):
            if dy == 0 and core is c:
                continue
            for k, src, dst in ((F_O, fos, fo.at[y, c]), (F_L, fls, fl.at[y, c])):
                cp = rc(k + n, src, dst, dev(dy=dy, core=core))
                cp.start()
                fback.append(cp)
                pend.append(cp)
            n += 1
    fo[y, c] = fos[...]
    fl[y, c] = fls[...]

    for cp in nback:
        cp.wait_recv()
    for cp in fback:
        cp.wait_recv()

    def spread(tile):
        return jnp.broadcast_to(tile[0:1], (128, 128)).T

    for h in range(HEADS):
        near_l = spread(nlr[h])
        far_l = [spread(fl[h, d]) for d in (0, 1)]
        near_o = nor[h].astype(F32)
        far_o = [fo[h, d].astype(F32) for d in (0, 1)]
        near_at = jnp.full((128, 128), nbk[h], jnp.int32)
        far_at = jnp.full((128, 128), foff[h], jnp.int32)
        for b in range(4):
            is_near = near_at == b
            is_far = far_at == lax.rem(seq, 8) * 4 + b
            ln = jnp.where(is_near, near_l, NEG)
            lf = [jnp.where(is_far, v, NEG) for v in far_l]
            l0 = ll[h, b]
            best = jnp.maximum(jnp.maximum(l0, ln), jnp.maximum(lf[0], lf[1]))
            w0 = jnp.exp(l0 - best)
            wn = jnp.exp(ln - best)
            wf = [jnp.exp(v - best) for v in lf]
            num = w0 * lo[h, b] + wn * near_o + wf[0] * far_o[0] + wf[1] * far_o[1]
            out[b * 128:b * 128 + 128, h * 128:h * 128 + 128] = (num / (w0 + wn + wf[0] + wf[1])).astype(BF)

    for cp in pend:
        cp.wait_send()

    @pl.when(odd)
    def _():
        nup.wait_send()

    @pl.when(even)
    def _():
        nupsib.wait_send()


def body(tokens, qkv_weight, near_offset, far_offset):
    vm = pltpu.VMEM
    mixed = pl.pallas_call(
        kernel,
        out_shape=jax.ShapeDtypeStruct((512, 512), BF),
        in_specs=[pl.BlockSpec(memory_space=pl.ANY)] * 2 + [pl.BlockSpec(memory_space=pltpu.SMEM)] * 2,
        out_specs=pl.BlockSpec(memory_space=pltpu.VMEM),
        scratch_shapes=[
            vm((4, 4, 512, 384), BF),
            vm((4, 512, 512), BF),
            vm((4, 512, 384), F32),
            vm((12, 8, 64, 128), BF),
            vm((4, 256, 128), BF),
            vm((4, 256, 128), BF),
            vm((4, 256, 128), BF),
            vm((4, 256, 128), BF),
            vm((16, 2, 64, 128), BF),
            vm((4, 128, 128), BF),
            vm((4, 2, 128, 128), BF),
            vm((4, 128, 128), BF),
            vm((2, 2, 4, 128, 128), BF),
            vm((2, 2, 4, 128, 128), BF),
            vm((4, 128, 128), F32),
            vm((4, 128, 128), F32),
            vm((4, 128, 128), F32),
            vm((4, 128, 128), BF),
            vm((4, 8, 128), F32),
            vm((4, 128, 128), BF),
            vm((4, 8, 128), F32),
            vm((128, 128), BF),
            vm((8, 128), F32),
            vm((4, 2, 128, 128), BF),
            vm((4, 2, 8, 128), F32),
            vm((4, 4, 128, 128), F32),
            vm((4, 4, 128, 128), F32),
            pltpu.SemaphoreType.DMA((N_SEM,)),
            pltpu.SemaphoreType.DMA((N_SEM,)),
            pltpu.SemaphoreType.DMA((8,)),
        ],
        compiler_params=pltpu.CompilerParams(
            collective_id=0, has_side_effects=True, vmem_limit_bytes=50 * 1024 * 1024),
    )(tokens[0], qkv_weight, near_offset, far_offset)
    return mixed[None]


def solution(mesh):
    in_specs = (P("fsdp", "seq", None), P("fsdp", None), P(), P())
    out_specs = P("fsdp", "seq", None)
    return jax.shard_map(body, mesh=mesh, in_specs=in_specs, out_specs=out_specs, check_vma=False)
```

```python
import jax
import jax.numpy as jnp
from jax import lax
from jax.experimental import pallas as pl
from jax.experimental.pallas import tpu as pltpu
from jax.sharding import PartitionSpec as P

HEADS = 4
HD = 128
NZ = 16
SCALE = HD ** (-0.5)
NEG = -1e30
BF = jnp.bfloat16
F32 = jnp.float32

X_W, SIDE, SIDE_Q, C_X, C_SIDE, C_QX, C_QSIDE = 0, 12, 24, 30, 34, 46, 48
F_KV, F_Q, N_Q, N_KV, N_SIB, N_UP, N_UPSIB = 54, 61, 68, 71, 74, 75, 76
R_UP, R_DN, N_O, N_L, F_O, F_L = 77, 85, 92, 95, 98, 105
N_SEM = 112


def qk(q, k):
    return lax.dot_general(q, k, (((1,), (1,)), ((), ())), preferred_element_type=F32) * SCALE


def pv(p, v):
    return jnp.dot(p.astype(BF), v, preferred_element_type=F32)


def lanes(column):
    return jnp.broadcast_to(column, (128, 128))


def kernel(tok, wgt, noff_h, foff_h, out, wk, wv, wq, tokv, acc, proj, fkvs, fqs, fkvc, fqc, kvf,
           nqs, nks, nq, nkv, ncross, nm, nl, no, nos, nls, nor, nlr, fos, fls, fo, fl, lo, ll,
           noff, foff, ssem, rsem, lsem):
    seq = lax.axis_index("seq")
    x = lax.axis_index("fsdp")
    z = lax.div(seq, 8)
    y = lax.rem(lax.div(seq, 2), 4)
    c = lax.rem(seq, 2)
    oc = 1 - c

    def dev(dx=0, dy=0, dz=0, core=c):
        return (lax.rem(z + dz, NZ) * 8 + lax.rem(y + dy, 4) * 2 + core, lax.rem(x + dx, 4))

    pend = []

    def rc(k, src, dst, to):
        return pltpu.make_async_remote_copy(
            src_ref=src, dst_ref=dst, send_sem=ssem.at[k], recv_sem=rsem.at[k],
            device_id=to, device_id_type=pl.DeviceIdType.MESH)

    def go(k, src, dst, to):
        cp = rc(k, src, dst, to)
        cp.start()
        pend.append(cp)
        return cp

    loads = [pltpu.make_async_copy(tok.at[:, pl.ds(512 * k, 512)], tokv.at[k], lsem.at[k]) for k in range(4)]
    loads.append(pltpu.make_async_copy(wgt.at[:, pl.ds(512, 512)], wk.at[0], lsem.at[4]))
    loads.append(pltpu.make_async_copy(wgt.at[:, pl.ds(1024, 512)], wv.at[0], lsem.at[5]))
    for n in (0, 1):
        loads.append(pltpu.make_async_copy(wgt.at[:, pl.ds(256 * n, 256)], wq.at[0, n], lsem.at[6 + n]))
    loads.append(pltpu.make_async_copy(noff_h, noff, lsem.at[8]))
    loads.append(pltpu.make_async_copy(foff_h, foff, lsem.at[9]))
    for ld in loads:
        ld.start()
    barrier = pltpu.get_barrier_semaphore()
    peers = [dev(dx=d) for d in (1, 2, 3)] + [dev(dz=d) for d in (1, 2, NZ - 2, NZ - 1)] + [dev(core=oc)]
    for dy in (1, 2, 3):
        peers += [dev(dy=dy), dev(dy=dy, core=oc)]
    for peer in peers:
        pl.semaphore_signal(barrier, inc=1, device_id=peer, device_id_type=pl.DeviceIdType.MESH)
    pl.semaphore_wait(barrier, len(peers))

    place = (y, lax.rem(z, 4))

    def strip(pos, core=c):
        return pl.ds(pl.multiple_of(128 * pos + 64 * core, 64), 64)

    def q_cols(n):
        return pl.ds(256 * n, 256)

    kv_w = (wk, wv)
    xw, xq = {}, {}
    for slot, dx in ((1, 3), (2, 1), (3, 2)):
        for n in (0, 1):
            r = strip(place[n])
            xw[n, slot] = go(X_W + n * 3 + slot - 1, wgt.at[r, pl.ds(512 + 512 * n, 512)],
                             kv_w[n].at[slot, r], dev(dx=dx))
    for slot, dx in ((1, 3), (2, 1), (3, 2)):
        for n in (0, 1):
            r = strip(place[n])
            xq[n, slot] = go(X_W + 6 + n * 3 + slot - 1, wgt.at[r, q_cols(n)], wq.at[slot, n, r], dev(dx=dx))

    for ld in loads:
        ld.wait()

    def tk(slot):
        return tokv[lax.rem(x + (0, 1, 3, 2)[slot], 4)]

    def dot(a, b):
        return jnp.dot(a, b, preferred_element_type=F32)

    for n in (0, 1):
        acc[n] = dot(tk(0), kv_w[n][0])
        acc[2, :, 256 * n:256 * n + 256] = dot(tk(0), wq[0, n])

    def side_dev(n, j):
        if n == 0:
            return dev(dy=j)
        return dev(dz=(1, 2 + (NZ - 4) * c, NZ - 1)[j - 1])

    groups = (pl.ds(1, 2), pl.ds(3, 1))
    sw, cx, cs = {}, {}, {}
    for g in (0, 1):
        for n in (0, 1):
            for slot in ((1, 2), (3,))[g]:
                xw[n, slot].wait_recv()
            part = kv_w[n].at[groups[g], strip(place[n])]
            for j in (1, 2, 3):
                sw[g, n, j] = go(SIDE + g * 6 + n * 3 + j - 1, part, part, side_dev(n, j))
            cx[g, n] = go(C_X + g * 2 + n, part, part, dev(core=oc))

    def arrived(n, j):
        return strip(lax.rem(place[n] + 4 - j, 4))

    def side_arrivals(g):
        for j in (1, 3, 2):
            for n in (0, 1):
                sw[g, n, j].wait_recv()
                part = kv_w[n].at[groups[g], arrived(n, j)]
                cs[g, n, j] = go(C_SIDE + g * 6 + n * 3 + j - 1, part, part, dev(core=oc))

    side_arrivals(0)
    sq, cq = {}, {}
    rest = pl.ds(1, 3)
    for n in (0, 1):
        for slot in (1, 2, 3):
            xq[n, slot].wait_recv()
        part = wq.at[rest, n, strip(place[n])]
        for j in (1, 2, 3):
            sq[n, j] = go(SIDE_Q + n * 3 + j - 1, part, part, side_dev(n, j))
        cq[n, 0] = go(C_QX + n, part, part, dev(core=oc))
    for n in (0, 1):
        cx[0, n].wait_recv()
        for j in (1, 3, 2):
            cs[0, n, j].wait_recv()
        acc[n] += dot(tk(1), kv_w[n][1]) + dot(tk(2), kv_w[n][2])
    side_arrivals(1)
    for n in (0, 1):
        cx[1, n].wait_recv()
        for j in (1, 3, 2):
            cs[1, n, j].wait_recv()
        r = acc[n] + dot(tk(3), kv_w[n][3])
        for h in range(HEADS):
            proj[4 + 4 * n + h] = r[:, 128 * h:128 * h + 128].astype(BF).reshape(8, 64, HD)

    def rows(j, b):
        return proj[j, pl.ds(2 * b, 2)].reshape(128, HD)

    def span(j, n, m):
        return proj[j, n // 64:m // 64].reshape(m - n, HD)

    fb = [lax.rem(foff[h], 4) for h in range(HEADS)]
    nbk = [noff[h] for h in range(HEADS)]
    for h in range(HEADS):
        for d in (0, 1):
            fkvs[d, h, 0] = proj[4 + h, 2 * fb[h] + d]
            fkvs[d, h, 1] = proj[8 + h, 2 * fb[h] + d]
    me = 2 * y + c
    fin = []
    for j in (0, 1, 2, 3):
        t = lax.rem(y + j, 4)
        for core in (c, oc):
            if j or core is oc:
                fin.append(go(F_KV + len(fin), fkvs.at[core, t], fkvc.at[me], dev(dy=j, core=core)))
    fkvc[me] = fkvs[c, y]
    for h in range(HEADS):
        nks[h, 0] = rows(4 + h, nbk[h])
        nks[h, 1] = rows(8 + h, nbk[h])
    nin = []
    for j in (1, 3, 2):
        t = lax.rem(y + j, 4)
        nin.append(go(N_KV + j - 1, nks.at[t], nkv.at[c, :, y], dev(dy=j)))
    nkv[c, 0, y] = nks[y, 0]
    nkv[c, 1, y] = nks[y, 1]

    for j in (1, 3, 2):
        for n in (0, 1):
            sq[n, j].wait_recv()
            part = wq.at[rest, n, arrived(n, j)]
            cq[n, j] = go(C_QSIDE + n * 3 + j - 1, part, part, dev(core=oc))

    for cp in fin:
        cp.wait_recv()
    holder = lax.div(foff[y], 4)
    kvf[0] = fkvc[holder]
    ups, dns = {}, {}

    def send_up(d, hops):
        ups[d] = go(R_UP + d - 1, kvf.at[d - hops], kvf.at[d], dev(dz=hops))

    def send_dn(d, hops):
        src = 0 if d == hops else 16 - d + hops
        dns[d] = go(R_DN + d - 1, kvf.at[src], kvf.at[16 - d], dev(dz=NZ - hops))

    def ring(d):
        if d:
            ups[d].wait_recv()
        send_up(d + 2, 2)
        if d:
            dns[d].wait_recv()
        if d < 6:
            send_dn(d + 2, 2)
        send_up(d + 1, 1)
        send_dn(d + 1, 1)

    ring(0)
    for cp in nin:
        cp.wait_recv()
    nsib = go(N_SIB, nkv.at[c], nkv.at[c], dev(core=oc))
    nup = rc(N_UP, nkv.at[c], ncross.at[c], dev(dz=1))
    odd = lax.rem(z, 2) == 1
    even = lax.rem(z, 2) == 0

    @pl.when(odd)
    def _():
        nup.start()

    for n in (0, 1):
        for j in (0, 1, 3, 2):
            cq[n, j].wait_recv()
        r = acc[2, :, 256 * n:256 * n + 256]
        for slot in (1, 2, 3):
            r = r + dot(tk(slot), wq[slot, n])
        for h in (0, 1):
            proj[2 * n + h] = r[:, 128 * h:128 * h + 128].astype(BF).reshape(8, 64, HD)
    for h in range(HEADS):
        fqs[h] = rows(h, fb[h])
        nqs[h] = rows(h, nbk[h])
    qin = []
    for j in (1, 3, 2):
        t = lax.rem(y + j, 4)
        qin.append(go(N_Q + j - 1, nqs.at[t], nq.at[y], dev(dy=j)))
    nq[y] = nqs[y]
    fqin = []
    for j in (0, 1, 2, 3):
        t = lax.rem(y + j, 4)
        for core in (c, oc):
            if j or core is oc:
                fqin.append(go(F_Q + len(fqin), fqs.at[t], fqc.at[me], dev(dy=j, core=core)))
    fqc[me] = fqs[y]

    qi = lax.broadcasted_iota(jnp.int32, (128, 128), 0)
    ki = lax.broadcasted_iota(jnp.int32, (128, 128), 1)
    causal = ki <= qi

    def local(h, i):
        n = 128 * i
        q = span(h, n, n + 128)
        s1 = jnp.where(causal, qk(q, span(4 + h, n, n + 128)), NEG)
        top = jnp.max(s1, axis=1, keepdims=True)
        if i:
            s0 = qk(q, span(4 + h, 0, n))
            top = jnp.maximum(top, jnp.max(s0, axis=1, keepdims=True))
        p1 = jnp.exp(s1 - top)
        tot = jnp.sum(p1, axis=1, keepdims=True)
        o = pv(p1, span(8 + h, n, n + 128))
        if i:
            p0 = jnp.exp(s0 - top)
            tot = tot + jnp.sum(p0, axis=1, keepdims=True)
            o = o + pv(p0, span(8 + h, 0, n))
        lo[h, i] = o / tot
        ll[h, i] = lanes(top + jnp.log(tot))

    for i in range(4):
        local(0, i)
    ring(2)
    for i in range(4):
        local(1, i)

    nsib.wait_recv()

    def near_plane(i):
        q = nq[i]
        m = 128 * (i + 1)
        sa = qk(q, nkv[c, 0, 0:i + 1].reshape(m, HD))
        sb = qk(q, nkv[oc, 0, 0:i + 1].reshape(m, HD))
        kk = lax.broadcasted_iota(jnp.int32, (128, m), 1)
        qq = lax.broadcasted_iota(jnp.int32, (128, m), 0) + 128 * i
        sa = jnp.where(kk <= qq, sa, NEG)
        sb = jnp.where(kk < 128 * (i + c), sb, NEG)
        top = jnp.maximum(jnp.max(sa, axis=1, keepdims=True), jnp.max(sb, axis=1, keepdims=True))
        pa = jnp.exp(sa - top)
        pb = jnp.exp(sb - top)
        tot = jnp.sum(pa, axis=1, keepdims=True) + jnp.sum(pb, axis=1, keepdims=True)
        no[i] = pv(pa, nkv[c, 1, 0:i + 1].reshape(m, HD)) + pv(pb, nkv[oc, 1, 0:i + 1].reshape(m, HD))
        nm[i] = lanes(top)
        nl[i] = lanes(tot)

    nupsib = rc(N_UPSIB, ncross.at[c], ncross.at[c], dev(core=oc))

    @pl.when(even)
    def _():
        nup.wait_recv()
        nupsib.start()

    for cp in qin:
        cp.wait_recv()
    near_plane(0)
    near_plane(1)
    ring(4)
    near_plane(2)
    near_plane(3)
    for i in range(4):
        local(2, i)

    @pl.when(even)
    def _():
        nupsib.wait_recv()

    def near_cross(i):
        q = nq[i]
        ss = [qk(q, ncross[d, 0].reshape(512, HD)) for d in (0, 1)]
        old = nm[i][:, 0:1]
        top = jnp.maximum(old, jnp.maximum(jnp.max(ss[0], axis=1, keepdims=True),
                                           jnp.max(ss[1], axis=1, keepdims=True)))
        w = jnp.exp(old - top)
        ps = [jnp.exp(s - top) for s in ss]
        tot = w * nl[i][:, 0:1] + jnp.sum(ps[0], axis=1, keepdims=True) + jnp.sum(ps[1], axis=1, keepdims=True)
        no[i] = w * no[i] + pv(ps[0], ncross[0, 1].reshape(512, HD)) + pv(ps[1], ncross[1, 1].reshape(512, HD))
        nm[i] = lanes(top)
        nl[i] = lanes(tot)

    cross = even & (z > 0)

    @pl.when(cross)
    def _():
        for i in range(4):
            near_cross(i)

    for i in range(4):
        nos[i] = (no[i] / nl[i]).astype(BF)
        nls[i] = (nm[i] + jnp.log(nl[i])).T[0:8]
    nback = []
    for j in (1, 2, 3):
        t = lax.rem(y + j, 4)
        for k, src, dst in ((N_O, nos.at[t], nor.at[y]), (N_L, nls.at[t], nlr.at[y])):
            nback.append(go(k + j - 1, src, dst, dev(dy=j)))
    nor[y] = nos[y]
    nlr[y] = nls[y]

    ring(6)
    for i in range(4):
        local(3, i)
    for cp in fqin:
        cp.wait_recv()
    for d in (1, 3, 5, 7, 8):
        ups[d].wait_recv()
        if d < 8:
            dns[d].wait_recv()

    sf = qk(fqc[holder], kvf[:, 0].reshape(1024, HD))
    kk = lax.broadcasted_iota(jnp.int32, (128, 1024), 1)
    qq = lax.broadcasted_iota(jnp.int32, (128, 1024), 0)
    dist = lax.shift_right_logical(kk, 6)
    seen = (dist <= z) & ((dist > 0) | (kk + 64 * c <= qq))
    sf = jnp.where(seen, sf, NEG)
    top = jnp.max(sf, axis=1, keepdims=True)
    pf = jnp.exp(sf - top)
    tot = jnp.sum(pf, axis=1, keepdims=True)
    fos[...] = (pv(pf, kvf[:, 1].reshape(1024, HD)) / tot).astype(BF)
    fls[...] = lanes(top + jnp.log(tot)).T[0:8]
    fback = []
    n = 0
    for dy in (1, 3, 2, 0):
        for core in (c, oc):
            if dy == 0 and core is c:
                continue
            for k, src, dst in ((F_O, fos, fo.at[y, c]), (F_L, fls, fl.at[y, c])):
                fback.append(go(k + n, src, dst, dev(dy=dy, core=core)))
            n += 1
    fo[y, c] = fos[...]
    fl[y, c] = fls[...]

    for cp in nback:
        cp.wait_recv()
    for cp in fback:
        cp.wait_recv()

    def spread(tile):
        return jnp.broadcast_to(tile[0:1], (128, 128)).T

    for h in range(HEADS):
        near_l = spread(nlr[h])
        far_l = [spread(fl[h, d]) for d in (0, 1)]
        near_o = nor[h].astype(F32)
        far_o = [fo[h, d].astype(F32) for d in (0, 1)]
        near_at = jnp.full((128, 128), nbk[h], jnp.int32)
        far_at = jnp.full((128, 128), foff[h], jnp.int32)
        for b in range(4):
            is_near = near_at == b
            is_far = far_at == lax.rem(seq, 8) * 4 + b
            ln = jnp.where(is_near, near_l, NEG)
            lf = [jnp.where(is_far, v, NEG) for v in far_l]
            l0 = ll[h, b]
            best = jnp.maximum(jnp.maximum(l0, ln), jnp.maximum(lf[0], lf[1]))
            w0 = jnp.exp(l0 - best)
            wn = jnp.exp(ln - best)
            wf = [jnp.exp(v - best) for v in lf]
            num = w0 * lo[h, b] + wn * near_o + wf[0] * far_o[0] + wf[1] * far_o[1]
            out[b * 128:b * 128 + 128, h * 128:h * 128 + 128] = (num / (w0 + wn + wf[0] + wf[1])).astype(BF)

    for cp in pend:
        cp.wait_send()

    @pl.when(odd)
    def _():
        nup.wait_send()

    @pl.when(even)
    def _():
        nupsib.wait_send()


def body(tokens, qkv_weight, near_offset, far_offset):
    vm = pltpu.VMEM
    mixed = pl.pallas_call(
        kernel,
        out_shape=jax.ShapeDtypeStruct((512, 512), BF),
        in_specs=[pl.BlockSpec(memory_space=pl.ANY)] * 4,
        out_specs=pl.BlockSpec(memory_space=pltpu.VMEM),
        scratch_shapes=[
            vm((4, 512, 512), BF),
            vm((4, 512, 512), BF),
            vm((4, 2, 512, 256), BF),
            vm((4, 512, 512), BF),
            vm((3, 512, 512), F32),
            vm((12, 8, 64, 128), BF),
            vm((2, 4, 2, 64, 128), BF),
            vm((4, 128, 128), BF),
            vm((8, 2, 64, 128), BF),
            vm((8, 128, 128), BF),
            vm((16, 2, 64, 128), BF),
            vm((4, 128, 128), BF),
            vm((4, 2, 128, 128), BF),
            vm((4, 128, 128), BF),
            vm((2, 2, 4, 128, 128), BF),
            vm((2, 2, 4, 128, 128), BF),
            vm((4, 128, 128), F32),
            vm((4, 128, 128), F32),
            vm((4, 128, 128), F32),
            vm((4, 128, 128), BF),
            vm((4, 8, 128), F32),
            vm((4, 128, 128), BF),
            vm((4, 8, 128), F32),
            vm((128, 128), BF),
            vm((8, 128), F32),
            vm((4, 2, 128, 128), BF),
            vm((4, 2, 8, 128), F32),
            vm((4, 4, 128, 128), F32),
            vm((4, 4, 128, 128), F32),
            pltpu.SMEM((4,), jnp.int32),
            pltpu.SMEM((4,), jnp.int32),
            pltpu.SemaphoreType.DMA((N_SEM,)),
            pltpu.SemaphoreType.DMA((N_SEM,)),
            pltpu.SemaphoreType.DMA((10,)),
        ],
        compiler_params=pltpu.CompilerParams(
            collective_id=0, has_side_effects=True, vmem_limit_bytes=60 * 1024 * 1024),
    )(tokens[0], qkv_weight, near_offset, far_offset)
    return mixed[None]


def solution(mesh):
    in_specs = (P("fsdp", "seq", None), P("fsdp", None), P(), P())
    out_specs = P("fsdp", "seq", None)
    return jax.shard_map(body, mesh=mesh, in_specs=in_specs, out_specs=out_specs, check_vma=False)
```

```python
import jax
import jax.numpy as jnp
from jax import lax
from jax.experimental import pallas as pl
from jax.experimental.pallas import tpu as pltpu
from jax.sharding import PartitionSpec as P

HEADS = 4
HD = 128
NZ = 16
SCALE = HD ** (-0.5)
NEG = -1e30
BF = jnp.bfloat16
F32 = jnp.float32

X_W, SIDE, SIDE_Q, C_X, C_SIDE, C_QX, C_QSIDE = 0, 12, 24, 30, 34, 46, 48
F_KV, F_Q, N_Q, N_KV, N_SIB, N_UP, N_UPSIB = 54, 61, 68, 71, 74, 75, 76
R_UP, R_DN, N_O, N_L, F_O, F_L = 77, 85, 92, 95, 98, 105
N_SEM = 112


def qk(q, k):
    return lax.dot_general(q, k, (((1,), (1,)), ((), ())), preferred_element_type=F32) * SCALE


def pv(p, v):
    return jnp.dot(p.astype(BF), v, preferred_element_type=F32)


def lanes(column):
    return jnp.broadcast_to(column, (128, 128))


def kernel(tok, wgt, noff_h, foff_h, out, wk, wv, wq, tokv, acc, proj, fkvs, fqs, fkvc, fqc, kvf,
           nqs, nks, nq, nkv, ncross, nm, nl, no, nos, nls, nor, nlr, fos, fls, fo, fl, lo, ll, nw,
           noff, foff, ssem, rsem, lsem):
    seq = lax.axis_index("seq")
    x = lax.axis_index("fsdp")
    z = lax.div(seq, 8)
    y = lax.rem(lax.div(seq, 2), 4)
    c = lax.rem(seq, 2)
    oc = 1 - c

    def dev(dx=0, dy=0, dz=0, core=c):
        return (lax.rem(z + dz, NZ) * 8 + lax.rem(y + dy, 4) * 2 + core, lax.rem(x + dx, 4))

    pend = []

    def rc(k, src, dst, to):
        return pltpu.make_async_remote_copy(
            src_ref=src, dst_ref=dst, send_sem=ssem.at[k], recv_sem=rsem.at[k],
            device_id=to, device_id_type=pl.DeviceIdType.MESH)

    def go(k, src, dst, to):
        cp = rc(k, src, dst, to)
        cp.start()
        pend.append(cp)
        return cp

    loads = [pltpu.make_async_copy(tok.at[:, pl.ds(512 * k, 512)], tokv.at[k], lsem.at[k]) for k in range(4)]
    loads.append(pltpu.make_async_copy(wgt.at[:, pl.ds(512, 512)], wk.at[0], lsem.at[4]))
    loads.append(pltpu.make_async_copy(wgt.at[:, pl.ds(1024, 512)], wv.at[0], lsem.at[5]))
    for n in (0, 1):
        loads.append(pltpu.make_async_copy(wgt.at[:, pl.ds(256 * n, 256)], wq.at[0, n], lsem.at[6 + n]))
    loads.append(pltpu.make_async_copy(noff_h, noff, lsem.at[8]))
    loads.append(pltpu.make_async_copy(foff_h, foff, lsem.at[9]))
    for ld in loads:
        ld.start()
    barrier = pltpu.get_barrier_semaphore()
    peers = [dev(dx=d) for d in (1, 2, 3)] + [dev(dz=d) for d in (1, 2, NZ - 2, NZ - 1)] + [dev(core=oc)]
    for dy in (1, 2, 3):
        peers += [dev(dy=dy), dev(dy=dy, core=oc)]
    for peer in peers:
        pl.semaphore_signal(barrier, inc=1, device_id=peer, device_id_type=pl.DeviceIdType.MESH)
    pl.semaphore_wait(barrier, len(peers))

    place = (y, lax.rem(z, 4))

    def strip(pos, core=c):
        return pl.ds(pl.multiple_of(128 * pos + 64 * core, 64), 64)

    def q_cols(n):
        return pl.ds(256 * n, 256)

    kv_w = (wk, wv)
    xw, xq = {}, {}
    for slot, dx in ((1, 3), (2, 1), (3, 2)):
        for n in (0, 1):
            r = strip(place[n])
            xw[n, slot] = go(X_W + n * 3 + slot - 1, wgt.at[r, pl.ds(512 + 512 * n, 512)],
                             kv_w[n].at[slot, r], dev(dx=dx))
    for slot, dx in ((1, 3), (2, 1), (3, 2)):
        for n in (0, 1):
            r = strip(place[n])
            xq[n, slot] = go(X_W + 6 + n * 3 + slot - 1, wgt.at[r, q_cols(n)], wq.at[slot, n, r], dev(dx=dx))

    for ld in loads:
        ld.wait()

    def tk(slot):
        return tokv[lax.rem(x + (0, 1, 3, 2)[slot], 4)]

    def dot(a, b):
        return jnp.dot(a, b, preferred_element_type=F32)

    for n in (0, 1):
        acc[n] = dot(tk(0), kv_w[n][0])
        acc[2, :, 256 * n:256 * n + 256] = dot(tk(0), wq[0, n])

    def side_dev(n, j):
        if n == 0:
            return dev(dy=j)
        return dev(dz=(1, 2 + (NZ - 4) * c, NZ - 1)[j - 1])

    groups = (pl.ds(1, 2), pl.ds(3, 1))
    sw, cx, cs = {}, {}, {}
    for g in (0, 1):
        for n in (0, 1):
            for slot in ((1, 2), (3,))[g]:
                xw[n, slot].wait_recv()
            part = kv_w[n].at[groups[g], strip(place[n])]
            for j in (1, 2, 3):
                sw[g, n, j] = go(SIDE + g * 6 + n * 3 + j - 1, part, part, side_dev(n, j))
            cx[g, n] = go(C_X + g * 2 + n, part, part, dev(core=oc))

    def arrived(n, j):
        return strip(lax.rem(place[n] + 4 - j, 4))

    def side_arrivals(g):
        for j in (1, 3, 2):
            for n in (0, 1):
                sw[g, n, j].wait_recv()
                part = kv_w[n].at[groups[g], arrived(n, j)]
                cs[g, n, j] = go(C_SIDE + g * 6 + n * 3 + j - 1, part, part, dev(core=oc))

    sq, cq = {}, {}
    rest = pl.ds(1, 3)
    for n in (0, 1):
        for slot in (1, 2, 3):
            xq[n, slot].wait_recv()
        part = wq.at[rest, n, strip(place[n])]
        for j in (1, 2, 3):
            sq[n, j] = go(SIDE_Q + n * 3 + j - 1, part, part, side_dev(n, j))
        cq[n, 0] = go(C_QX + n, part, part, dev(core=oc))
    side_arrivals(0)
    for n in (0, 1):
        cx[0, n].wait_recv()
        for j in (1, 3, 2):
            cs[0, n, j].wait_recv()
        acc[n] += dot(tk(1), kv_w[n][1]) + dot(tk(2), kv_w[n][2])
    side_arrivals(1)
    for n in (0, 1):
        cx[1, n].wait_recv()
        for j in (1, 3, 2):
            cs[1, n, j].wait_recv()
        r = acc[n] + dot(tk(3), kv_w[n][3])
        for h in range(HEADS):
            proj[4 + 4 * n + h] = r[:, 128 * h:128 * h + 128].astype(BF).reshape(8, 64, HD)

    def rows(j, b):
        return proj[j, pl.ds(2 * b, 2)].reshape(128, HD)

    def span(j, n, m):
        return proj[j, n // 64:m // 64].reshape(m - n, HD)

    fb = [lax.rem(foff[h], 4) for h in range(HEADS)]
    nbk = [noff[h] for h in range(HEADS)]
    for h in range(HEADS):
        for d in (0, 1):
            fkvs[d, h, 0] = proj[4 + h, 2 * fb[h] + d]
            fkvs[d, h, 1] = proj[8 + h, 2 * fb[h] + d]
    me = 2 * y + c
    fin = []
    for j in (0, 1, 2, 3):
        t = lax.rem(y + j, 4)
        for core in (c, oc):
            if j or core is oc:
                fin.append(go(F_KV + len(fin), fkvs.at[core, t], fkvc.at[me], dev(dy=j, core=core)))
    fkvc[me] = fkvs[c, y]
    for h in range(HEADS):
        nks[h, 0] = rows(4 + h, nbk[h])
        nks[h, 1] = rows(8 + h, nbk[h])
    nin = []
    for j in (1, 3, 2):
        t = lax.rem(y + j, 4)
        nin.append(go(N_KV + j - 1, nks.at[t], nkv.at[c, :, y], dev(dy=j)))
    nkv[c, 0, y] = nks[y, 0]
    nkv[c, 1, y] = nks[y, 1]

    for j in (1, 3, 2):
        for n in (0, 1):
            sq[n, j].wait_recv()
            part = wq.at[rest, n, arrived(n, j)]
            cq[n, j] = go(C_QSIDE + n * 3 + j - 1, part, part, dev(core=oc))

    for cp in fin:
        cp.wait_recv()
    holder = lax.div(foff[y], 4)
    kvf[0] = fkvc[holder]
    ups, dns = {}, {}

    def send_up(d, hops):
        ups[d] = go(R_UP + d - 1, kvf.at[d - hops], kvf.at[d], dev(dz=hops))

    def send_dn(d, hops):
        src = 0 if d == hops else 16 - d + hops
        dns[d] = go(R_DN + d - 1, kvf.at[src], kvf.at[16 - d], dev(dz=NZ - hops))

    def ring(d):
        if d:
            ups[d].wait_recv()
        send_up(d + 2, 2)
        if d:
            dns[d].wait_recv()
        if d < 6:
            send_dn(d + 2, 2)
        send_up(d + 1, 1)
        send_dn(d + 1, 1)

    ring(0)
    for cp in nin:
        cp.wait_recv()
    nsib = go(N_SIB, nkv.at[c], nkv.at[c], dev(core=oc))
    nup = rc(N_UP, nkv.at[c], ncross.at[c], dev(dz=1))
    odd = lax.rem(z, 2) == 1
    even = lax.rem(z, 2) == 0

    @pl.when(odd)
    def _():
        nup.start()

    for n in (0, 1):
        for j in (0, 1, 3, 2):
            cq[n, j].wait_recv()
        r = acc[2, :, 256 * n:256 * n + 256]
        for slot in (1, 2, 3):
            r = r + dot(tk(slot), wq[slot, n])
        for h in (0, 1):
            proj[2 * n + h] = r[:, 128 * h:128 * h + 128].astype(BF).reshape(8, 64, HD)
    for h in range(HEADS):
        fqs[h] = rows(h, fb[h])
        nqs[h] = rows(h, nbk[h])
    qin = []
    for j in (1, 3, 2):
        t = lax.rem(y + j, 4)
        qin.append(go(N_Q + j - 1, nqs.at[t], nq.at[y], dev(dy=j)))
    nq[y] = nqs[y]
    fqin = []
    for j in (0, 1, 2, 3):
        t = lax.rem(y + j, 4)
        for core in (c, oc):
            if j or core is oc:
                fqin.append(go(F_Q + len(fqin), fqs.at[t], fqc.at[me], dev(dy=j, core=core)))
    fqc[me] = fqs[y]

    qi = lax.broadcasted_iota(jnp.int32, (128, 128), 0)
    ki = lax.broadcasted_iota(jnp.int32, (128, 128), 1)
    causal = ki <= qi

    def local(h, i):
        n = 128 * i
        q = span(h, n, n + 128)
        s1 = jnp.where(causal, qk(q, span(4 + h, n, n + 128)), NEG)
        top = jnp.max(s1, axis=1, keepdims=True)
        if i:
            s0 = qk(q, span(4 + h, 0, n))
            top = jnp.maximum(top, jnp.max(s0, axis=1, keepdims=True))
        p1 = jnp.exp(s1 - top)
        tot = jnp.sum(p1, axis=1, keepdims=True)
        o = pv(p1, span(8 + h, n, n + 128))
        if i:
            p0 = jnp.exp(s0 - top)
            tot = tot + jnp.sum(p0, axis=1, keepdims=True)
            o = o + pv(p0, span(8 + h, 0, n))
        lo[h, i] = o / tot
        ll[h, i] = lanes(top + jnp.log(tot))

    ring(2)
    for h in (0, 1):
        for i in range(4):
            local(h, i)
    ring(4)
    for h in (2, 3):
        for i in range(4):
            local(h, i)

    nsib.wait_recv()

    def near_plane(i):
        q = nq[i]
        m = 128 * (i + 1)
        sa = qk(q, nkv[c, 0, 0:i + 1].reshape(m, HD))
        sb = qk(q, nkv[oc, 0, 0:i + 1].reshape(m, HD))
        kk = lax.broadcasted_iota(jnp.int32, (128, m), 1)
        qq = lax.broadcasted_iota(jnp.int32, (128, m), 0) + 128 * i
        sa = jnp.where(kk <= qq, sa, NEG)
        sb = jnp.where(kk < 128 * (i + c), sb, NEG)
        top = jnp.maximum(jnp.max(sa, axis=1, keepdims=True), jnp.max(sb, axis=1, keepdims=True))
        pa = jnp.exp(sa - top)
        pb = jnp.exp(sb - top)
        tot = jnp.sum(pa, axis=1, keepdims=True) + jnp.sum(pb, axis=1, keepdims=True)
        no[i] = pv(pa, nkv[c, 1, 0:i + 1].reshape(m, HD)) + pv(pb, nkv[oc, 1, 0:i + 1].reshape(m, HD))
        nm[i] = lanes(top)
        nl[i] = lanes(tot)

    for cp in qin:
        cp.wait_recv()
    near_plane(0)
    near_plane(1)
    ring(6)
    nupsib = rc(N_UPSIB, ncross.at[c], ncross.at[c], dev(core=oc))

    @pl.when(even)
    def _():
        nup.wait_recv()
        nupsib.start()

    near_plane(2)
    near_plane(3)

    @pl.when(even)
    def _():
        nupsib.wait_recv()

    def near_cross(i):
        q = nq[i]
        ss = [qk(q, ncross[d, 0].reshape(512, HD)) for d in (0, 1)]
        old = nm[i][:, 0:1]
        top = jnp.maximum(old, jnp.maximum(jnp.max(ss[0], axis=1, keepdims=True),
                                           jnp.max(ss[1], axis=1, keepdims=True)))
        w = jnp.exp(old - top)
        ps = [jnp.exp(s - top) for s in ss]
        tot = w * nl[i][:, 0:1] + jnp.sum(ps[0], axis=1, keepdims=True) + jnp.sum(ps[1], axis=1, keepdims=True)
        no[i] = w * no[i] + pv(ps[0], ncross[0, 1].reshape(512, HD)) + pv(ps[1], ncross[1, 1].reshape(512, HD))
        nm[i] = lanes(top)
        nl[i] = lanes(tot)

    cross = even & (z > 0)

    @pl.when(cross)
    def _():
        for i in range(4):
            near_cross(i)

    for i in range(4):
        nos[i] = (no[i] / nl[i]).astype(BF)
        nls[i] = (nm[i] + jnp.log(nl[i])).T[0:8]
    nback = []
    for j in (1, 2, 3):
        t = lax.rem(y + j, 4)
        for k, src, dst in ((N_O, nos.at[t], nor.at[y]), (N_L, nls.at[t], nlr.at[y])):
            nback.append(go(k + j - 1, src, dst, dev(dy=j)))
    nor[y] = nos[y]
    nlr[y] = nls[y]

    for cp in fqin:
        cp.wait_recv()
    for d in (1, 3, 5, 7, 8):
        ups[d].wait_recv()
        if d < 8:
            dns[d].wait_recv()

    sf = qk(fqc[holder], kvf[:, 0].reshape(1024, HD))
    kk = lax.broadcasted_iota(jnp.int32, (128, 1024), 1)
    qq = lax.broadcasted_iota(jnp.int32, (128, 1024), 0)
    dist = lax.shift_right_logical(kk, 6)
    seen = (dist <= z) & ((dist > 0) | (kk + 64 * c <= qq))
    sf = jnp.where(seen, sf, NEG)
    top = jnp.max(sf, axis=1, keepdims=True)
    pf = jnp.exp(sf - top)
    tot = jnp.sum(pf, axis=1, keepdims=True)
    fos[...] = (pv(pf, kvf[:, 1].reshape(1024, HD)) / tot).astype(BF)
    fls[...] = lanes(top + jnp.log(tot)).T[0:8]
    fback = []
    n = 0
    for dy in (1, 3, 2, 0):
        for core in (c, oc):
            if dy == 0 and core is c:
                continue
            for k, src, dst in ((F_O, fos, fo.at[y, c]), (F_L, fls, fl.at[y, c])):
                fback.append(go(k + n, src, dst, dev(dy=dy, core=core)))
            n += 1
    fo[y, c] = fos[...]
    fl[y, c] = fls[...]

    def spread(tile):
        return jnp.broadcast_to(tile[0:1], (128, 128)).T

    for cp in nback:
        cp.wait_recv()
    for h in range(HEADS):
        near_l = spread(nlr[h])
        near_o = nor[h].astype(F32)
        near_at = jnp.full((128, 128), nbk[h], jnp.int32)
        for b in range(4):
            ln = jnp.where(near_at == b, near_l, NEG)
            l0 = ll[h, b]
            best = jnp.maximum(l0, ln)
            w0 = jnp.exp(l0 - best)
            wn = jnp.exp(ln - best)
            lo[h, b] = w0 * lo[h, b] + wn * near_o
            nw[h, b] = w0 + wn
            ll[h, b] = best
    for cp in fback:
        cp.wait_recv()
    for h in range(HEADS):
        far_l = [spread(fl[h, d]) for d in (0, 1)]
        far_o = [fo[h, d].astype(F32) for d in (0, 1)]
        far_at = jnp.full((128, 128), foff[h], jnp.int32)
        for b in range(4):
            is_far = far_at == lax.rem(seq, 8) * 4 + b
            lf = [jnp.where(is_far, v, NEG) for v in far_l]
            l0 = ll[h, b]
            best = jnp.maximum(l0, jnp.maximum(lf[0], lf[1]))
            w0 = jnp.exp(l0 - best)
            wf = [jnp.exp(v - best) for v in lf]
            num = w0 * lo[h, b] + wf[0] * far_o[0] + wf[1] * far_o[1]
            out[b * 128:b * 128 + 128, h * 128:h * 128 + 128] = (num / (w0 * nw[h, b] + wf[0] + wf[1])).astype(BF)

    for cp in pend:
        cp.wait_send()

    @pl.when(odd)
    def _():
        nup.wait_send()

    @pl.when(even)
    def _():
        nupsib.wait_send()


def body(tokens, qkv_weight, near_offset, far_offset):
    vm = pltpu.VMEM
    mixed = pl.pallas_call(
        kernel,
        out_shape=jax.ShapeDtypeStruct((512, 512), BF),
        in_specs=[pl.BlockSpec(memory_space=pl.ANY)] * 4,
        out_specs=pl.BlockSpec(memory_space=pltpu.VMEM),
        scratch_shapes=[
            vm((4, 512, 512), BF),
            vm((4, 512, 512), BF),
            vm((4, 2, 512, 256), BF),
            vm((4, 512, 512), BF),
            vm((3, 512, 512), F32),
            vm((12, 8, 64, 128), BF),
            vm((2, 4, 2, 64, 128), BF),
            vm((4, 128, 128), BF),
            vm((8, 2, 64, 128), BF),
            vm((8, 128, 128), BF),
            vm((16, 2, 64, 128), BF),
            vm((4, 128, 128), BF),
            vm((4, 2, 128, 128), BF),
            vm((4, 128, 128), BF),
            vm((2, 2, 4, 128, 128), BF),
            vm((2, 2, 4, 128, 128), BF),
            vm((4, 128, 128), F32),
            vm((4, 128, 128), F32),
            vm((4, 128, 128), F32),
            vm((4, 128, 128), BF),
            vm((4, 8, 128), F32),
            vm((4, 128, 128), BF),
            vm((4, 8, 128), F32),
            vm((128, 128), BF),
            vm((8, 128), F32),
            vm((4, 2, 128, 128), BF),
            vm((4, 2, 8, 128), F32),
            vm((4, 4, 128, 128), F32),
            vm((4, 4, 128, 128), F32),
            vm((4, 4, 128, 128), F32),
            pltpu.SMEM((4,), jnp.int32),
            pltpu.SMEM((4,), jnp.int32),
            pltpu.SemaphoreType.DMA((N_SEM,)),
            pltpu.SemaphoreType.DMA((N_SEM,)),
            pltpu.SemaphoreType.DMA((10,)),
        ],
        compiler_params=pltpu.CompilerParams(
            collective_id=0, has_side_effects=True, vmem_limit_bytes=60 * 1024 * 1024),
    )(tokens[0], qkv_weight, near_offset, far_offset)
    return mixed[None]


def solution(mesh):
    in_specs = (P("fsdp", "seq", None), P("fsdp", None), P(), P())
    out_specs = P("fsdp", "seq", None)
    return jax.shard_map(body, mesh=mesh, in_specs=in_specs, out_specs=out_specs, check_vma=False)
```

```python
import jax
import jax.numpy as jnp
from jax import lax
from jax.experimental import pallas as pl
from jax.experimental.pallas import tpu as pltpu
from jax.sharding import PartitionSpec as P

HEADS = 4
HD = 128
NZ = 16
SCALE = HD ** (-0.5)
NEG = -1e30
BF = jnp.bfloat16
F32 = jnp.float32

X_W, X_Q, SIDE, C_X, C_SIDE, C_Q = 0, 6, 9, 21, 25, 37
F_KV, F_Q, N_Q, N_KV, N_SIB, N_UP, N_UPSIB = 40, 47, 54, 57, 60, 61, 62
R_UP, R_DN, N_O, F_O = 63, 71, 78, 81
N_SEM = 88


def qk(q, k):
    return lax.dot_general(q, k, (((1,), (1,)), ((), ())), preferred_element_type=F32) * SCALE


def pv(p, v):
    return jnp.dot(p.astype(BF), v, preferred_element_type=F32)


def lanes(column):
    return jnp.broadcast_to(column, (128, 128))


def kernel(tok, wgt, noff_h, foff_h, out, wk, wv, wq, tokv, acc, proj, fkvs, fqs, fkvc, fqc, kvf,
           nqs, nks, nq, nkv, ncross, nm, nl, no, nos, nor, fos, fo, lo, ll, nw,
           noff, foff, ssem, rsem, lsem):
    seq = lax.axis_index("seq")
    x = lax.axis_index("fsdp")
    z = lax.div(seq, 8)
    y = lax.rem(lax.div(seq, 2), 4)
    c = lax.rem(seq, 2)
    oc = 1 - c

    def dev(dx=0, dy=0, dz=0, core=c):
        return (lax.rem(z + dz, NZ) * 8 + lax.rem(y + dy, 4) * 2 + core, lax.rem(x + dx, 4))

    pend = []

    def rc(k, src, dst, to):
        return pltpu.make_async_remote_copy(
            src_ref=src, dst_ref=dst, send_sem=ssem.at[k], recv_sem=rsem.at[k],
            device_id=to, device_id_type=pl.DeviceIdType.MESH)

    def go(k, src, dst, to):
        cp = rc(k, src, dst, to)
        cp.start()
        pend.append(cp)
        return cp

    loads = [pltpu.make_async_copy(tok.at[:, pl.ds(512 * k, 512)], tokv.at[k], lsem.at[k]) for k in range(4)]
    loads.append(pltpu.make_async_copy(wgt.at[:, pl.ds(512, 512)], wk.at[0], lsem.at[4]))
    loads.append(pltpu.make_async_copy(wgt.at[:, pl.ds(1024, 512)], wv.at[0], lsem.at[5]))
    loads.append(pltpu.make_async_copy(wgt.at[:, pl.ds(0, 512)], wq.at[0], lsem.at[6]))
    loads.append(pltpu.make_async_copy(noff_h, noff, lsem.at[7]))
    loads.append(pltpu.make_async_copy(foff_h, foff, lsem.at[8]))
    for ld in loads:
        ld.start()
    barrier = pltpu.get_barrier_semaphore()
    peers = [dev(dx=d) for d in (1, 2, 3)] + [dev(dz=d) for d in (1, 2, NZ - 2, NZ - 1)] + [dev(core=oc)]
    for dy in (1, 2, 3):
        peers += [dev(dy=dy), dev(dy=dy, core=oc)]
    for peer in peers:
        pl.semaphore_signal(barrier, inc=1, device_id=peer, device_id_type=pl.DeviceIdType.MESH)
    pl.semaphore_wait(barrier, len(peers))

    place = (y, lax.rem(z, 4))

    def strip(pos, core=c):
        return pl.ds(pl.multiple_of(128 * pos + 64 * core, 64), 64)

    kv_w = (wk, wv)
    xw, xq = {}, {}
    for slot, dx in ((1, 3), (2, 1), (3, 2)):
        for n in (0, 1):
            r = strip(place[n])
            xw[n, slot] = go(X_W + n * 3 + slot - 1, wgt.at[r, pl.ds(512 + 512 * n, 512)],
                             kv_w[n].at[slot, r], dev(dx=dx))
    half = pl.ds(pl.multiple_of(256 * c, 256), 256)
    for slot, dx in ((1, 3), (2, 1), (3, 2)):
        xq[slot] = go(X_Q + slot - 1, wgt.at[half, pl.ds(0, 512)], wq.at[slot, half], dev(dx=dx))

    for ld in loads:
        ld.wait()

    def tk(slot):
        return tokv[lax.rem(x + (0, 1, 3, 2)[slot], 4)]

    def dot(a, b):
        return jnp.dot(a, b, preferred_element_type=F32)

    for n in (0, 1):
        acc[n] = dot(tk(0), kv_w[n][0])
    acc[2] = dot(tk(0), wq[0])

    def side_dev(n, j):
        if n == 0:
            return dev(dy=j)
        return dev(dz=(1, 2 + (NZ - 4) * c, NZ - 1)[j - 1])

    groups = (pl.ds(1, 2), pl.ds(3, 1))
    sw, cx, cs = {}, {}, {}
    for g in (0, 1):
        for n in (0, 1):
            for slot in ((1, 2), (3,))[g]:
                xw[n, slot].wait_recv()
            part = kv_w[n].at[groups[g], strip(place[n])]
            for j in (1, 2, 3):
                sw[g, n, j] = go(SIDE + g * 6 + n * 3 + j - 1, part, part, side_dev(n, j))
            cx[g, n] = go(C_X + g * 2 + n, part, part, dev(core=oc))

    def arrived(n, j):
        return strip(lax.rem(place[n] + 4 - j, 4))

    def side_arrivals(g):
        for j in (1, 3, 2):
            for n in (0, 1):
                sw[g, n, j].wait_recv()
                part = kv_w[n].at[groups[g], arrived(n, j)]
                cs[g, n, j] = go(C_SIDE + g * 6 + n * 3 + j - 1, part, part, dev(core=oc))

    side_arrivals(0)
    for n in (0, 1):
        cx[0, n].wait_recv()
        for j in (1, 3, 2):
            cs[0, n, j].wait_recv()
        acc[n] += dot(tk(1), kv_w[n][1]) + dot(tk(2), kv_w[n][2])
    side_arrivals(1)
    for n in (0, 1):
        cx[1, n].wait_recv()
        for j in (1, 3, 2):
            cs[1, n, j].wait_recv()
        r = acc[n] + dot(tk(3), kv_w[n][3])
        for h in range(HEADS):
            proj[4 + 4 * n + h] = r[:, 128 * h:128 * h + 128].astype(BF).reshape(8, 64, HD)

    def rows(j, b):
        return proj[j, pl.ds(2 * b, 2)].reshape(128, HD)

    def span(j, n, m):
        return proj[j, n // 64:m // 64].reshape(m - n, HD)

    fb = [lax.rem(foff[h], 4) for h in range(HEADS)]
    nbk = [noff[h] for h in range(HEADS)]
    for h in range(HEADS):
        for d in (0, 1):
            fkvs[d, h, 0] = proj[4 + h, 2 * fb[h] + d]
            fkvs[d, h, 1] = proj[8 + h, 2 * fb[h] + d]
    me = 2 * y + c
    fin = []
    for j in (0, 1, 2, 3):
        t = lax.rem(y + j, 4)
        for core in (c, oc):
            if j or core is oc:
                fin.append(go(F_KV + len(fin), fkvs.at[core, t], fkvc.at[me], dev(dy=j, core=core)))
    fkvc[me] = fkvs[c, y]
    for h in range(HEADS):
        nks[h, 0] = rows(4 + h, nbk[h])
        nks[h, 1] = rows(8 + h, nbk[h])
    nin = []
    for j in (1, 3, 2):
        t = lax.rem(y + j, 4)
        nin.append(go(N_KV + j - 1, nks.at[t], nkv.at[c, :, y], dev(dy=j)))
    nkv[c, 0, y] = nks[y, 0]
    nkv[c, 1, y] = nks[y, 1]

    cq = {}
    for slot in (1, 2, 3):
        xq[slot].wait_recv()
        cq[slot] = go(C_Q + slot - 1, wq.at[slot, half], wq.at[slot, half], dev(core=oc))

    for cp in fin:
        cp.wait_recv()
    holder = lax.div(foff[y], 4)
    kvf[0] = fkvc[holder]
    ups, dns = {}, {}

    def send_up(d, hops):
        ups[d] = go(R_UP + d - 1, kvf.at[d - hops], kvf.at[d], dev(dz=hops))

    def send_dn(d, hops):
        src = 0 if d == hops else 16 - d + hops
        dns[d] = go(R_DN + d - 1, kvf.at[src], kvf.at[16 - d], dev(dz=NZ - hops))

    def ring(d):
        if d:
            ups[d].wait_recv()
        send_up(d + 2, 2)
        if d:
            dns[d].wait_recv()
        if d < 6:
            send_dn(d + 2, 2)
        send_up(d + 1, 1)
        send_dn(d + 1, 1)

    ring(0)
    for cp in nin:
        cp.wait_recv()
    nsib = go(N_SIB, nkv.at[c], nkv.at[c], dev(core=oc))
    nup = rc(N_UP, nkv.at[c], ncross.at[c], dev(dz=1))
    odd = lax.rem(z, 2) == 1
    even = lax.rem(z, 2) == 0

    @pl.when(odd)
    def _():
        nup.start()

    for slot in (1, 2, 3):
        cq[slot].wait_recv()
    r = acc[2] + dot(tk(1), wq[1]) + dot(tk(2), wq[2]) + dot(tk(3), wq[3])
    for h in range(HEADS):
        proj[h] = r[:, 128 * h:128 * h + 128].astype(BF).reshape(8, 64, HD)
    ring(2)
    for h in range(HEADS):
        fqs[h] = rows(h, fb[h])
        nqs[h] = rows(h, nbk[h])
    qin = []
    for j in (1, 3, 2):
        t = lax.rem(y + j, 4)
        qin.append(go(N_Q + j - 1, nqs.at[t], nq.at[y], dev(dy=j)))
    nq[y] = nqs[y]
    fqin = []
    for j in (0, 1, 2, 3):
        t = lax.rem(y + j, 4)
        for core in (c, oc):
            if j or core is oc:
                fqin.append(go(F_Q + len(fqin), fqs.at[t], fqc.at[me], dev(dy=j, core=core)))
    fqc[me] = fqs[y]

    def pack(lse):
        t = lse.T[0:16]
        a = t.astype(BF).astype(F32)
        b = (t - a).astype(BF).astype(F32)
        row = lax.broadcasted_iota(jnp.int32, (16, 128), 0)
        return jnp.where(row == 0, a, jnp.where(row == 1, b, t - a - b)).astype(BF)

    qi = lax.broadcasted_iota(jnp.int32, (128, 128), 0)
    ki = lax.broadcasted_iota(jnp.int32, (128, 128), 1)
    causal = ki <= qi

    def local(h, i):
        n = 128 * i
        q = span(h, n, n + 128)
        s1 = jnp.where(causal, qk(q, span(4 + h, n, n + 128)), NEG)
        top = jnp.max(s1, axis=1, keepdims=True)
        if i:
            s0 = qk(q, span(4 + h, 0, n))
            top = jnp.maximum(top, jnp.max(s0, axis=1, keepdims=True))
        p1 = jnp.exp(s1 - top)
        tot = jnp.sum(p1, axis=1, keepdims=True)
        o = pv(p1, span(8 + h, n, n + 128))
        if i:
            p0 = jnp.exp(s0 - top)
            tot = tot + jnp.sum(p0, axis=1, keepdims=True)
            o = o + pv(p0, span(8 + h, 0, n))
        lo[h, i] = o / tot
        ll[h, i] = lanes(top + jnp.log(tot))

    for h in (0, 1):
        for i in range(4):
            local(h, i)
    ring(4)
    for h in (2, 3):
        for i in range(4):
            local(h, i)

    nsib.wait_recv()

    def near_plane(i):
        q = nq[i]
        m = 128 * (i + 1)
        sa = qk(q, nkv[c, 0, 0:i + 1].reshape(m, HD))
        sb = qk(q, nkv[oc, 0, 0:i + 1].reshape(m, HD))
        kk = lax.broadcasted_iota(jnp.int32, (128, m), 1)
        qq = lax.broadcasted_iota(jnp.int32, (128, m), 0) + 128 * i
        sa = jnp.where(kk <= qq, sa, NEG)
        sb = jnp.where(kk < 128 * (i + c), sb, NEG)
        top = jnp.maximum(jnp.max(sa, axis=1, keepdims=True), jnp.max(sb, axis=1, keepdims=True))
        pa = jnp.exp(sa - top)
        pb = jnp.exp(sb - top)
        tot = jnp.sum(pa, axis=1, keepdims=True) + jnp.sum(pb, axis=1, keepdims=True)
        no[i] = pv(pa, nkv[c, 1, 0:i + 1].reshape(m, HD)) + pv(pb, nkv[oc, 1, 0:i + 1].reshape(m, HD))
        nm[i] = lanes(top)
        nl[i] = lanes(tot)

    for cp in qin:
        cp.wait_recv()
    near_plane(0)
    near_plane(1)
    ring(6)
    nupsib = rc(N_UPSIB, ncross.at[c], ncross.at[c], dev(core=oc))

    @pl.when(even)
    def _():
        nup.wait_recv()
        nupsib.start()

    near_plane(2)
    near_plane(3)

    @pl.when(even)
    def _():
        nupsib.wait_recv()

    def near_cross(i):
        q = nq[i]
        ss = [qk(q, ncross[d, 0].reshape(512, HD)) for d in (0, 1)]
        old = nm[i][:, 0:1]
        top = jnp.maximum(old, jnp.maximum(jnp.max(ss[0], axis=1, keepdims=True),
                                           jnp.max(ss[1], axis=1, keepdims=True)))
        w = jnp.exp(old - top)
        ps = [jnp.exp(s - top) for s in ss]
        tot = w * nl[i][:, 0:1] + jnp.sum(ps[0], axis=1, keepdims=True) + jnp.sum(ps[1], axis=1, keepdims=True)
        no[i] = w * no[i] + pv(ps[0], ncross[0, 1].reshape(512, HD)) + pv(ps[1], ncross[1, 1].reshape(512, HD))
        nm[i] = lanes(top)
        nl[i] = lanes(tot)

    cross = even & (z > 0)

    @pl.when(cross)
    def _():
        for i in range(4):
            near_cross(i)

    for i in range(4):
        nos[i, 0:128] = (no[i] / nl[i]).astype(BF)
        nos[i, 128:144] = pack(nm[i] + jnp.log(nl[i]))
    nback = []
    for j in (1, 2, 3):
        t = lax.rem(y + j, 4)
        nback.append(go(N_O + j - 1, nos.at[t], nor.at[y], dev(dy=j)))
    nor[y] = nos[y]

    for cp in fqin:
        cp.wait_recv()
    for d in (1, 3, 5, 7, 8):
        ups[d].wait_recv()
        if d < 8:
            dns[d].wait_recv()

    sf = qk(fqc[holder], kvf[:, 0].reshape(1024, HD))
    kk = lax.broadcasted_iota(jnp.int32, (128, 1024), 1)
    qq = lax.broadcasted_iota(jnp.int32, (128, 1024), 0)
    dist = lax.shift_right_logical(kk, 6)
    seen = (dist <= z) & ((dist > 0) | (kk + 64 * c <= qq))
    sf = jnp.where(seen, sf, NEG)
    top = jnp.max(sf, axis=1, keepdims=True)
    pf = jnp.exp(sf - top)
    tot = jnp.sum(pf, axis=1, keepdims=True)
    fos[0:128] = (pv(pf, kvf[:, 1].reshape(1024, HD)) / tot).astype(BF)
    fos[128:144] = pack(lanes(top + jnp.log(tot)))
    fback = []
    n = 0
    for dy in (1, 3, 2, 0):
        for core in (c, oc):
            if dy == 0 and core is c:
                continue
            fback.append(go(F_O + n, fos, fo.at[y, c], dev(dy=dy, core=core)))
            n += 1
    fo[y, c] = fos[...]

    def spread(tile):
        t = tile.astype(F32)
        return jnp.broadcast_to(t[0:1] + t[1:2] + t[2:3], (128, 128)).T

    for cp in nback:
        cp.wait_recv()
    for h in range(HEADS):
        near_l = spread(nor[h, 128:144])
        near_o = nor[h, 0:128].astype(F32)
        near_at = jnp.full((128, 128), nbk[h], jnp.int32)
        for b in range(4):
            ln = jnp.where(near_at == b, near_l, NEG)
            l0 = ll[h, b]
            best = jnp.maximum(l0, ln)
            w0 = jnp.exp(l0 - best)
            wn = jnp.exp(ln - best)
            lo[h, b] = w0 * lo[h, b] + wn * near_o
            nw[h, b] = w0 + wn
            ll[h, b] = best
    for cp in fback:
        cp.wait_recv()
    for h in range(HEADS):
        far_l = [spread(fo[h, d, 128:144]) for d in (0, 1)]
        far_o = [fo[h, d, 0:128].astype(F32) for d in (0, 1)]
        far_at = jnp.full((128, 128), foff[h], jnp.int32)
        for b in range(4):
            is_far = far_at == lax.rem(seq, 8) * 4 + b
            lf = [jnp.where(is_far, v, NEG) for v in far_l]
            l0 = ll[h, b]
            best = jnp.maximum(l0, jnp.maximum(lf[0], lf[1]))
            w0 = jnp.exp(l0 - best)
            wf = [jnp.exp(v - best) for v in lf]
            num = w0 * lo[h, b] + wf[0] * far_o[0] + wf[1] * far_o[1]
            out[b * 128:b * 128 + 128, h * 128:h * 128 + 128] = (num / (w0 * nw[h, b] + wf[0] + wf[1])).astype(BF)

    for cp in pend:
        cp.wait_send()

    @pl.when(odd)
    def _():
        nup.wait_send()

    @pl.when(even)
    def _():
        nupsib.wait_send()


def body(tokens, qkv_weight, near_offset, far_offset):
    vm = pltpu.VMEM
    mixed = pl.pallas_call(
        kernel,
        out_shape=jax.ShapeDtypeStruct((512, 512), BF),
        in_specs=[pl.BlockSpec(memory_space=pl.ANY)] * 4,
        out_specs=pl.BlockSpec(memory_space=pltpu.VMEM),
        scratch_shapes=[
            vm((4, 512, 512), BF),
            vm((4, 512, 512), BF),
            vm((4, 512, 512), BF),
            vm((4, 512, 512), BF),
            vm((3, 512, 512), F32),
            vm((12, 8, 64, 128), BF),
            vm((2, 4, 2, 64, 128), BF),
            vm((4, 128, 128), BF),
            vm((8, 2, 64, 128), BF),
            vm((8, 128, 128), BF),
            vm((16, 2, 64, 128), BF),
            vm((4, 128, 128), BF),
            vm((4, 2, 128, 128), BF),
            vm((4, 128, 128), BF),
            vm((2, 2, 4, 128, 128), BF),
            vm((2, 2, 4, 128, 128), BF),
            vm((4, 128, 128), F32),
            vm((4, 128, 128), F32),
            vm((4, 128, 128), F32),
            vm((4, 144, 128), BF),
            vm((4, 144, 128), BF),
            vm((144, 128), BF),
            vm((4, 2, 144, 128), BF),
            vm((4, 4, 128, 128), F32),
            vm((4, 4, 128, 128), F32),
            vm((4, 4, 128, 128), F32),
            pltpu.SMEM((4,), jnp.int32),
            pltpu.SMEM((4,), jnp.int32),
            pltpu.SemaphoreType.DMA((N_SEM,)),
            pltpu.SemaphoreType.DMA((N_SEM,)),
            pltpu.SemaphoreType.DMA((9,)),
        ],
        compiler_params=pltpu.CompilerParams(
            collective_id=0, has_side_effects=True, vmem_limit_bytes=60 * 1024 * 1024),
    )(tokens[0], qkv_weight, near_offset, far_offset)
    return mixed[None]


def solution(mesh):
    in_specs = (P("fsdp", "seq", None), P("fsdp", None), P(), P())
    out_specs = P("fsdp", "seq", None)
    return jax.shard_map(body, mesh=mesh, in_specs=in_specs, out_specs=out_specs, check_vma=False)
```

```python
import jax
import jax.numpy as jnp
from jax import lax
from jax.experimental import pallas as pl
from jax.experimental.pallas import tpu as pltpu
from jax.sharding import PartitionSpec as P

HEADS = 4
HD = 128
NZ = 16
SCALE = HD ** (-0.5)
NEG = -1e30
BF = jnp.bfloat16
F32 = jnp.float32

X_W, X_Q, SIDE, C_X, C_SIDE, C_Q = 0, 6, 9, 21, 25, 37
F_KV, F_Q, N_Q, N_KV, N_SIB, N_UP, N_UPSIB = 40, 47, 54, 57, 60, 61, 62
R_UP, R_DN, N_O, F_O = 63, 71, 78, 81
N_SEM = 88


def qk(q, k):
    return lax.dot_general(q, k, (((1,), (1,)), ((), ())), preferred_element_type=F32) * SCALE


def pv(p, v):
    return jnp.dot(p.astype(BF), v, preferred_element_type=F32)


def lanes(column):
    return jnp.broadcast_to(column, (128, 128))


def kernel(tok, wgt, noff_h, foff_h, out, wk, wv, wq, tokv, acc, proj, fkvs, fqs, fkvc, fqc, kvf,
           nqs, nks, nq, nkv, ncross, nm, nl, no, nos, nor, fos, fo, lo, ll, nw,
           noff, foff, ssem, rsem, lsem):
    seq = lax.axis_index("seq")
    x = lax.axis_index("fsdp")
    z = lax.div(seq, 8)
    y = lax.rem(lax.div(seq, 2), 4)
    c = lax.rem(seq, 2)
    oc = 1 - c

    def dev(dx=0, dy=0, dz=0, core=c):
        return (lax.rem(z + dz, NZ) * 8 + lax.rem(y + dy, 4) * 2 + core, lax.rem(x + dx, 4))

    pend = []

    def rc(k, src, dst, to):
        return pltpu.make_async_remote_copy(
            src_ref=src, dst_ref=dst, send_sem=ssem.at[k], recv_sem=rsem.at[k],
            device_id=to, device_id_type=pl.DeviceIdType.MESH)

    def go(k, src, dst, to):
        cp = rc(k, src, dst, to)
        cp.start()
        pend.append(cp)
        return cp

    loads = [pltpu.make_async_copy(tok.at[:, pl.ds(512 * k, 512)], tokv.at[k], lsem.at[k]) for k in range(4)]
    loads.append(pltpu.make_async_copy(wgt.at[:, pl.ds(512, 512)], wk.at[0], lsem.at[4]))
    loads.append(pltpu.make_async_copy(wgt.at[:, pl.ds(1024, 512)], wv.at[0], lsem.at[5]))
    loads.append(pltpu.make_async_copy(wgt.at[:, pl.ds(0, 512)], wq.at[0], lsem.at[6]))
    loads.append(pltpu.make_async_copy(noff_h, noff, lsem.at[7]))
    loads.append(pltpu.make_async_copy(foff_h, foff, lsem.at[8]))
    for ld in loads:
        ld.start()
    barrier = pltpu.get_barrier_semaphore()
    peers = [dev(dx=d) for d in (1, 2, 3)] + [dev(dz=d) for d in (1, 2, 3, 6, NZ - 6, NZ - 3, NZ - 2, NZ - 1)] + [dev(core=oc)]
    for dy in (1, 2, 3):
        peers += [dev(dy=dy), dev(dy=dy, core=oc)]
    for peer in peers:
        pl.semaphore_signal(barrier, inc=1, device_id=peer, device_id_type=pl.DeviceIdType.MESH)
    pl.semaphore_wait(barrier, len(peers))

    place = (y, lax.rem(z, 4))

    def strip(pos, core=c):
        return pl.ds(pl.multiple_of(128 * pos + 64 * core, 64), 64)

    kv_w = (wk, wv)
    xw, xq = {}, {}
    for slot, dx in ((1, 3), (2, 1), (3, 2)):
        for n in (0, 1):
            r = strip(place[n])
            xw[n, slot] = go(X_W + n * 3 + slot - 1, wgt.at[r, pl.ds(512 + 512 * n, 512)],
                             kv_w[n].at[slot, r], dev(dx=dx))
    half = pl.ds(pl.multiple_of(256 * c, 256), 256)
    for slot, dx in ((1, 3), (2, 1), (3, 2)):
        xq[slot] = go(X_Q + slot - 1, wgt.at[half, pl.ds(0, 512)], wq.at[slot, half], dev(dx=dx))

    for ld in loads:
        ld.wait()

    def tk(slot):
        return tokv[lax.rem(x + (0, 1, 3, 2)[slot], 4)]

    def dot(a, b):
        return jnp.dot(a, b, preferred_element_type=F32)

    for n in (0, 1):
        acc[n] = dot(tk(0), kv_w[n][0])
    acc[2] = dot(tk(0), wq[0])

    def side_dev(n, j):
        if n == 0:
            return dev(dy=j)
        return dev(dz=(1, 2 + (NZ - 4) * c, NZ - 1)[j - 1])

    groups = (pl.ds(1, 2), pl.ds(3, 1))
    sw, cx, cs = {}, {}, {}
    for g in (0, 1):
        for n in (0, 1):
            for slot in ((1, 2), (3,))[g]:
                xw[n, slot].wait_recv()
            part = kv_w[n].at[groups[g], strip(place[n])]
            for j in (1, 2, 3):
                sw[g, n, j] = go(SIDE + g * 6 + n * 3 + j - 1, part, part, side_dev(n, j))
            cx[g, n] = go(C_X + g * 2 + n, part, part, dev(core=oc))

    def arrived(n, j):
        return strip(lax.rem(place[n] + 4 - j, 4))

    def side_arrivals(g):
        for j in (1, 3, 2):
            for n in (0, 1):
                sw[g, n, j].wait_recv()
                part = kv_w[n].at[groups[g], arrived(n, j)]
                cs[g, n, j] = go(C_SIDE + g * 6 + n * 3 + j - 1, part, part, dev(core=oc))

    side_arrivals(0)
    for n in (0, 1):
        cx[0, n].wait_recv()
        for j in (1, 3, 2):
            cs[0, n, j].wait_recv()
        acc[n] += dot(tk(1), kv_w[n][1]) + dot(tk(2), kv_w[n][2])
    side_arrivals(1)
    for n in (0, 1):
        cx[1, n].wait_recv()
        for j in (1, 3, 2):
            cs[1, n, j].wait_recv()
        r = acc[n] + dot(tk(3), kv_w[n][3])
        for h in range(HEADS):
            proj[4 + 4 * n + h] = r[:, 128 * h:128 * h + 128].astype(BF).reshape(8, 64, HD)

    def rows(j, b):
        return proj[j, pl.ds(2 * b, 2)].reshape(128, HD)

    def span(j, n, m):
        return proj[j, n // 64:m // 64].reshape(m - n, HD)

    fb = [lax.rem(foff[h], 4) for h in range(HEADS)]
    nbk = [noff[h] for h in range(HEADS)]
    for h in range(HEADS):
        for d in (0, 1):
            fkvs[d, h, 0] = proj[4 + h, 2 * fb[h] + d]
            fkvs[d, h, 1] = proj[8 + h, 2 * fb[h] + d]
    me = 2 * y + c
    fin = []
    for j in (0, 1, 2, 3):
        t = lax.rem(y + j, 4)
        for core in (c, oc):
            if j or core is oc:
                fin.append(go(F_KV + len(fin), fkvs.at[core, t], fkvc.at[me], dev(dy=j, core=core)))
    fkvc[me] = fkvs[c, y]

    cq = {}
    for slot in (1, 2, 3):
        xq[slot].wait_recv()
        cq[slot] = go(C_Q + slot - 1, wq.at[slot, half], wq.at[slot, half], dev(core=oc))

    for cp in fin:
        cp.wait_recv()
    holder = lax.div(foff[y], 4)
    kvf[0] = fkvc[holder]
    ups, dns = {}, {}

    def send_up(d, hops):
        ups[d] = go(R_UP + d - 1, kvf.at[d - hops], kvf.at[d], dev(dz=hops))

    def send_dn(d, hops):
        src = 0 if d == hops else 16 - d + hops
        dns[d] = go(R_DN + d - 1, kvf.at[src], kvf.at[16 - d], dev(dz=NZ - hops))

    for d in (6, 3, 2, 1):
        send_up(d, d)
        send_dn(d, d)

    def relay(d):
        ups[d].wait_recv()
        send_up(d + 2, 2)
        dns[d].wait_recv()
        if d == 3:
            send_dn(d + 2, 2)
        send_up(d + 1, 1)
        send_dn(d + 1, 1)

    for h in range(HEADS):
        nks[h, 0] = rows(4 + h, nbk[h])
        nks[h, 1] = rows(8 + h, nbk[h])
    nin = []
    for j in (1, 3, 2):
        t = lax.rem(y + j, 4)
        nin.append(go(N_KV + j - 1, nks.at[t], nkv.at[c, :, y], dev(dy=j)))
    nkv[c, 0, y] = nks[y, 0]
    nkv[c, 1, y] = nks[y, 1]

    for slot in (1, 2, 3):
        cq[slot].wait_recv()
    r = acc[2] + dot(tk(1), wq[1]) + dot(tk(2), wq[2]) + dot(tk(3), wq[3])
    for h in range(HEADS):
        proj[h] = r[:, 128 * h:128 * h + 128].astype(BF).reshape(8, 64, HD)
    for h in range(HEADS):
        fqs[h] = rows(h, fb[h])
        nqs[h] = rows(h, nbk[h])
    qin = []
    for j in (1, 3, 2):
        t = lax.rem(y + j, 4)
        qin.append(go(N_Q + j - 1, nqs.at[t], nq.at[y], dev(dy=j)))
    nq[y] = nqs[y]
    fqin = []
    for j in (0, 1, 2, 3):
        t = lax.rem(y + j, 4)
        for core in (c, oc):
            if j or core is oc:
                fqin.append(go(F_Q + len(fqin), fqs.at[t], fqc.at[me], dev(dy=j, core=core)))
    fqc[me] = fqs[y]
    relay(3)
    for cp in nin:
        cp.wait_recv()
    nsib = go(N_SIB, nkv.at[c], nkv.at[c], dev(core=oc))
    nup = rc(N_UP, nkv.at[c], ncross.at[c], dev(dz=1))
    odd = lax.rem(z, 2) == 1
    even = lax.rem(z, 2) == 0

    @pl.when(odd)
    def _():
        nup.start()
    relay(6)

    def pack(lse):
        t = lse.T[0:16]
        a = t.astype(BF).astype(F32)
        b = (t - a).astype(BF).astype(F32)
        row = lax.broadcasted_iota(jnp.int32, (16, 128), 0)
        return jnp.where(row == 0, a, jnp.where(row == 1, b, t - a - b)).astype(BF)

    qi = lax.broadcasted_iota(jnp.int32, (128, 128), 0)
    ki = lax.broadcasted_iota(jnp.int32, (128, 128), 1)
    causal = ki <= qi

    def local(h, i):
        n = 128 * i
        q = span(h, n, n + 128)
        s1 = jnp.where(causal, qk(q, span(4 + h, n, n + 128)), NEG)
        top = jnp.max(s1, axis=1, keepdims=True)
        if i:
            s0 = qk(q, span(4 + h, 0, n))
            top = jnp.maximum(top, jnp.max(s0, axis=1, keepdims=True))
        p1 = jnp.exp(s1 - top)
        tot = jnp.sum(p1, axis=1, keepdims=True)
        o = pv(p1, span(8 + h, n, n + 128))
        if i:
            p0 = jnp.exp(s0 - top)
            tot = tot + jnp.sum(p0, axis=1, keepdims=True)
            o = o + pv(p0, span(8 + h, 0, n))
        lo[h, i] = o / tot
        ll[h, i] = lanes(top + jnp.log(tot))

    for h in (0, 1, 2):
        for i in range(4):
            local(h, i)

    nupsib = rc(N_UPSIB, ncross.at[c], ncross.at[c], dev(core=oc))

    @pl.when(even)
    def _():
        nup.wait_recv()
        nupsib.start()

    for i in range(4):
        local(3, i)

    nsib.wait_recv()

    def near_plane(i):
        q = nq[i]
        m = 128 * (i + 1)
        sa = qk(q, nkv[c, 0, 0:i + 1].reshape(m, HD))
        sb = qk(q, nkv[oc, 0, 0:i + 1].reshape(m, HD))
        kk = lax.broadcasted_iota(jnp.int32, (128, m), 1)
        qq = lax.broadcasted_iota(jnp.int32, (128, m), 0) + 128 * i
        sa = jnp.where(kk <= qq, sa, NEG)
        sb = jnp.where(kk < 128 * (i + c), sb, NEG)
        top = jnp.maximum(jnp.max(sa, axis=1, keepdims=True), jnp.max(sb, axis=1, keepdims=True))
        pa = jnp.exp(sa - top)
        pb = jnp.exp(sb - top)
        tot = jnp.sum(pa, axis=1, keepdims=True) + jnp.sum(pb, axis=1, keepdims=True)
        no[i] = pv(pa, nkv[c, 1, 0:i + 1].reshape(m, HD)) + pv(pb, nkv[oc, 1, 0:i + 1].reshape(m, HD))
        nm[i] = lanes(top)
        nl[i] = lanes(tot)

    for cp in qin:
        cp.wait_recv()
    near_plane(0)
    near_plane(1)
    near_plane(2)
    near_plane(3)

    @pl.when(even)
    def _():
        nupsib.wait_recv()

    def near_cross(i):
        q = nq[i]
        ss = [qk(q, ncross[d, 0].reshape(512, HD)) for d in (0, 1)]
        old = nm[i][:, 0:1]
        top = jnp.maximum(old, jnp.maximum(jnp.max(ss[0], axis=1, keepdims=True),
                                           jnp.max(ss[1], axis=1, keepdims=True)))
        w = jnp.exp(old - top)
        ps = [jnp.exp(s - top) for s in ss]
        tot = w * nl[i][:, 0:1] + jnp.sum(ps[0], axis=1, keepdims=True) + jnp.sum(ps[1], axis=1, keepdims=True)
        no[i] = w * no[i] + pv(ps[0], ncross[0, 1].reshape(512, HD)) + pv(ps[1], ncross[1, 1].reshape(512, HD))
        nm[i] = lanes(top)
        nl[i] = lanes(tot)

    cross = even & (z > 0)

    @pl.when(cross)
    def _():
        for i in range(4):
            near_cross(i)

    for i in range(4):
        nos[i, 0:128] = (no[i] / nl[i]).astype(BF)
        nos[i, 128:144] = pack(nm[i] + jnp.log(nl[i]))
    nback = []
    for j in (1, 2, 3):
        t = lax.rem(y + j, 4)
        nback.append(go(N_O + j - 1, nos.at[t], nor.at[y], dev(dy=j)))
    nor[y] = nos[y]

    for cp in fqin:
        cp.wait_recv()
    for d in (1, 2, 4, 5, 7, 8):
        ups[d].wait_recv()
        if d < 8:
            dns[d].wait_recv()

    sf = qk(fqc[holder], kvf[:, 0].reshape(1024, HD))
    kk = lax.broadcasted_iota(jnp.int32, (128, 1024), 1)
    qq = lax.broadcasted_iota(jnp.int32, (128, 1024), 0)
    dist = lax.shift_right_logical(kk, 6)
    seen = (dist <= z) & ((dist > 0) | (kk + 64 * c <= qq))
    sf = jnp.where(seen, sf, NEG)
    top = jnp.max(sf, axis=1, keepdims=True)
    pf = jnp.exp(sf - top)
    tot = jnp.sum(pf, axis=1, keepdims=True)
    fos[0:128] = (pv(pf, kvf[:, 1].reshape(1024, HD)) / tot).astype(BF)
    fos[128:144] = pack(lanes(top + jnp.log(tot)))
    fback = []
    n = 0
    for dy in (1, 3, 2, 0):
        for core in (c, oc):
            if dy == 0 and core is c:
                continue
            fback.append(go(F_O + n, fos, fo.at[y, c], dev(dy=dy, core=core)))
            n += 1
    fo[y, c] = fos[...]

    def spread(tile):
        t = tile.astype(F32)
        return jnp.broadcast_to(t[0:1] + t[1:2] + t[2:3], (128, 128)).T

    for cp in nback:
        cp.wait_recv()
    for h in range(HEADS):
        near_l = spread(nor[h, 128:144])
        near_o = nor[h, 0:128].astype(F32)
        near_at = jnp.full((128, 128), nbk[h], jnp.int32)
        for b in range(4):
            ln = jnp.where(near_at == b, near_l, NEG)
            l0 = ll[h, b]
            best = jnp.maximum(l0, ln)
            w0 = jnp.exp(l0 - best)
            wn = jnp.exp(ln - best)
            lo[h, b] = w0 * lo[h, b] + wn * near_o
            nw[h, b] = w0 + wn
            ll[h, b] = best
    for cp in fback:
        cp.wait_recv()
    for h in range(HEADS):
        far_l = [spread(fo[h, d, 128:144]) for d in (0, 1)]
        far_o = [fo[h, d, 0:128].astype(F32) for d in (0, 1)]
        far_at = jnp.full((128, 128), foff[h], jnp.int32)
        for b in range(4):
            is_far = far_at == lax.rem(seq, 8) * 4 + b
            lf = [jnp.where(is_far, v, NEG) for v in far_l]
            l0 = ll[h, b]
            best = jnp.maximum(l0, jnp.maximum(lf[0], lf[1]))
            w0 = jnp.exp(l0 - best)
            wf = [jnp.exp(v - best) for v in lf]
            num = w0 * lo[h, b] + wf[0] * far_o[0] + wf[1] * far_o[1]
            out[b * 128:b * 128 + 128, h * 128:h * 128 + 128] = (num / (w0 * nw[h, b] + wf[0] + wf[1])).astype(BF)

    for cp in pend:
        cp.wait_send()

    @pl.when(odd)
    def _():
        nup.wait_send()

    @pl.when(even)
    def _():
        nupsib.wait_send()


def body(tokens, qkv_weight, near_offset, far_offset):
    vm = pltpu.VMEM
    mixed = pl.pallas_call(
        kernel,
        out_shape=jax.ShapeDtypeStruct((512, 512), BF),
        in_specs=[pl.BlockSpec(memory_space=pl.ANY)] * 4,
        out_specs=pl.BlockSpec(memory_space=pltpu.VMEM),
        scratch_shapes=[
            vm((4, 512, 512), BF),
            vm((4, 512, 512), BF),
            vm((4, 512, 512), BF),
            vm((4, 512, 512), BF),
            vm((3, 512, 512), F32),
            vm((12, 8, 64, 128), BF),
            vm((2, 4, 2, 64, 128), BF),
            vm((4, 128, 128), BF),
            vm((8, 2, 64, 128), BF),
            vm((8, 128, 128), BF),
            vm((16, 2, 64, 128), BF),
            vm((4, 128, 128), BF),
            vm((4, 2, 128, 128), BF),
            vm((4, 128, 128), BF),
            vm((2, 2, 4, 128, 128), BF),
            vm((2, 2, 4, 128, 128), BF),
            vm((4, 128, 128), F32),
            vm((4, 128, 128), F32),
            vm((4, 128, 128), F32),
            vm((4, 144, 128), BF),
            vm((4, 144, 128), BF),
            vm((144, 128), BF),
            vm((4, 2, 144, 128), BF),
            vm((4, 4, 128, 128), F32),
            vm((4, 4, 128, 128), F32),
            vm((4, 4, 128, 128), F32),
            pltpu.SMEM((4,), jnp.int32),
            pltpu.SMEM((4,), jnp.int32),
            pltpu.SemaphoreType.DMA((N_SEM,)),
            pltpu.SemaphoreType.DMA((N_SEM,)),
            pltpu.SemaphoreType.DMA((9,)),
        ],
        compiler_params=pltpu.CompilerParams(
            collective_id=0, has_side_effects=True, vmem_limit_bytes=60 * 1024 * 1024),
    )(tokens[0], qkv_weight, near_offset, far_offset)
    return mixed[None]


def solution(mesh):
    in_specs = (P("fsdp", "seq", None), P("fsdp", None), P(), P())
    out_specs = P("fsdp", "seq", None)
    return jax.shard_map(body, mesh=mesh, in_specs=in_specs, out_specs=out_specs, check_vma=False)
```

```python
import jax
import jax.numpy as jnp
from jax import lax
from jax.experimental import pallas as pl
from jax.experimental.pallas import tpu as pltpu
from jax.sharding import PartitionSpec as P

HEADS = 4
HD = 128
NZ = 16
SCALE = HD ** (-0.5)
NEG = -1e30
BF = jnp.bfloat16
F32 = jnp.float32

X_W, X_Q, SIDE, C_X, C_SIDE, C_Q = 0, 6, 9, 21, 25, 37
F_KV, F_Q, N_Q, N_KV, N_SIB = 40, 47, 54, 57, 60
R_UP, R_DN, N_O, F_O, N_QD, N_OC = 61, 69, 76, 79, 86, 90
N_SEM = 94


def qk(q, k):
    return lax.dot_general(q, k, (((1,), (1,)), ((), ())), preferred_element_type=F32) * SCALE


def pv(p, v):
    return jnp.dot(p.astype(BF), v, preferred_element_type=F32)


def lanes(column):
    return jnp.broadcast_to(column, (128, 128))


def kernel(tok, wgt, noff_h, foff_h, out, wk, wv, wq, tokv, acc, proj, fkvs, fqs, fkvc, fqc, kvf,
           nqs, nks, nq, nkv, ncq, cos, cor, nos, nor, fos, fo, lo, ll, nw,
           noff, foff, ssem, rsem, lsem):
    seq = lax.axis_index("seq")
    x = lax.axis_index("fsdp")
    z = lax.div(seq, 8)
    y = lax.rem(lax.div(seq, 2), 4)
    c = lax.rem(seq, 2)
    oc = 1 - c

    def dev(dx=0, dy=0, dz=0, core=c):
        return (lax.rem(z + dz, NZ) * 8 + lax.rem(y + dy, 4) * 2 + core, lax.rem(x + dx, 4))

    pend = []

    def rc(k, src, dst, to):
        return pltpu.make_async_remote_copy(
            src_ref=src, dst_ref=dst, send_sem=ssem.at[k], recv_sem=rsem.at[k],
            device_id=to, device_id_type=pl.DeviceIdType.MESH)

    def go(k, src, dst, to):
        cp = rc(k, src, dst, to)
        cp.start()
        pend.append(cp)
        return cp

    loads = [pltpu.make_async_copy(tok.at[:, pl.ds(512 * k, 512)], tokv.at[k], lsem.at[k]) for k in range(4)]
    loads.append(pltpu.make_async_copy(wgt.at[:, pl.ds(512, 512)], wk.at[0], lsem.at[4]))
    loads.append(pltpu.make_async_copy(wgt.at[:, pl.ds(1024, 512)], wv.at[0], lsem.at[5]))
    loads.append(pltpu.make_async_copy(wgt.at[:, pl.ds(0, 512)], wq.at[0], lsem.at[6]))
    loads.append(pltpu.make_async_copy(noff_h, noff, lsem.at[7]))
    loads.append(pltpu.make_async_copy(foff_h, foff, lsem.at[8]))
    for ld in loads:
        ld.start()
    barrier = pltpu.get_barrier_semaphore()
    peers = [dev(dx=d) for d in (1, 2, 3)] + [dev(dz=d) for d in (1, 2, NZ - 2, NZ - 1)] + [dev(core=oc)]
    for dy in (1, 2, 3):
        peers += [dev(dy=dy), dev(dy=dy, core=oc), dev(dy=dy, dz=1), dev(dy=dy, dz=NZ - 1)]
    for peer in peers:
        pl.semaphore_signal(barrier, inc=1, device_id=peer, device_id_type=pl.DeviceIdType.MESH)
    pl.semaphore_wait(barrier, len(peers))

    place = (y, lax.rem(z, 4))

    def strip(pos, core=c):
        return pl.ds(pl.multiple_of(128 * pos + 64 * core, 64), 64)

    kv_w = (wk, wv)
    xw, xq = {}, {}
    for slot, dx in ((1, 3), (2, 1), (3, 2)):
        for n in (0, 1):
            r = strip(place[n])
            xw[n, slot] = go(X_W + n * 3 + slot - 1, wgt.at[r, pl.ds(512 + 512 * n, 512)],
                             kv_w[n].at[slot, r], dev(dx=dx))
    half = pl.ds(pl.multiple_of(256 * c, 256), 256)
    for slot, dx in ((1, 3), (2, 1), (3, 2)):
        xq[slot] = go(X_Q + slot - 1, wgt.at[half, pl.ds(0, 512)], wq.at[slot, half], dev(dx=dx))

    for ld in loads:
        ld.wait()

    def tk(slot):
        return tokv[lax.rem(x + (0, 1, 3, 2)[slot], 4)]

    def dot(a, b):
        return jnp.dot(a, b, preferred_element_type=F32)

    for n in (0, 1):
        acc[n] = dot(tk(0), kv_w[n][0])
    acc[2] = dot(tk(0), wq[0])

    def side_dev(n, j):
        if n == 0:
            return dev(dy=j)
        return dev(dz=(1, 2 + (NZ - 4) * c, NZ - 1)[j - 1])

    groups = (pl.ds(1, 2), pl.ds(3, 1))
    sw, cx, cs = {}, {}, {}
    for g in (0, 1):
        for n in (0, 1):
            for slot in ((1, 2), (3,))[g]:
                xw[n, slot].wait_recv()
            part = kv_w[n].at[groups[g], strip(place[n])]
            for j in (1, 2, 3):
                sw[g, n, j] = go(SIDE + g * 6 + n * 3 + j - 1, part, part, side_dev(n, j))
            cx[g, n] = go(C_X + g * 2 + n, part, part, dev(core=oc))

    def arrived(n, j):
        return strip(lax.rem(place[n] + 4 - j, 4))

    def side_arrivals(g):
        for j in (1, 3, 2):
            for n in (0, 1):
                sw[g, n, j].wait_recv()
                part = kv_w[n].at[groups[g], arrived(n, j)]
                cs[g, n, j] = go(C_SIDE + g * 6 + n * 3 + j - 1, part, part, dev(core=oc))

    side_arrivals(0)
    for n in (0, 1):
        cx[0, n].wait_recv()
        for j in (1, 3, 2):
            cs[0, n, j].wait_recv()
        acc[n] += dot(tk(1), kv_w[n][1]) + dot(tk(2), kv_w[n][2])
    side_arrivals(1)
    for n in (0, 1):
        cx[1, n].wait_recv()
        for j in (1, 3, 2):
            cs[1, n, j].wait_recv()
        r = acc[n] + dot(tk(3), kv_w[n][3])
        for h in range(HEADS):
            proj[4 + 4 * n + h] = r[:, 128 * h:128 * h + 128].astype(BF).reshape(8, 64, HD)

    def rows(j, b):
        return proj[j, pl.ds(2 * b, 2)].reshape(128, HD)

    def span(j, n, m):
        return proj[j, n // 64:m // 64].reshape(m - n, HD)

    fb = [lax.rem(foff[h], 4) for h in range(HEADS)]
    nbk = [noff[h] for h in range(HEADS)]
    for h in range(HEADS):
        for d in (0, 1):
            fkvs[d, h, 0] = proj[4 + h, 2 * fb[h] + d]
            fkvs[d, h, 1] = proj[8 + h, 2 * fb[h] + d]
    me = 2 * y + c
    fin = []
    for j in (0, 1, 2, 3):
        t = lax.rem(y + j, 4)
        for core in (c, oc):
            if j or core is oc:
                fin.append(go(F_KV + len(fin), fkvs.at[core, t], fkvc.at[me], dev(dy=j, core=core)))
    fkvc[me] = fkvs[c, y]
    for h in range(HEADS):
        nks[h, 0] = rows(4 + h, nbk[h])
        nks[h, 1] = rows(8 + h, nbk[h])
    nin = []
    for j in (1, 3, 2):
        t = lax.rem(y + j, 4)
        nin.append(go(N_KV + j - 1, nks.at[t], nkv.at[c, :, y], dev(dy=j)))
    nkv[c, 0, y] = nks[y, 0]
    nkv[c, 1, y] = nks[y, 1]

    cq = {}
    for slot in (1, 2, 3):
        xq[slot].wait_recv()
        cq[slot] = go(C_Q + slot - 1, wq.at[slot, half], wq.at[slot, half], dev(core=oc))

    for cp in fin:
        cp.wait_recv()
    holder = lax.div(foff[y], 4)
    kvf[0] = fkvc[holder]
    ups, dns = {}, {}

    def send_up(d, hops):
        ups[d] = go(R_UP + d - 1, kvf.at[d - hops], kvf.at[d], dev(dz=hops))

    def send_dn(d, hops):
        src = 0 if d == hops else 16 - d + hops
        dns[d] = go(R_DN + d - 1, kvf.at[src], kvf.at[16 - d], dev(dz=NZ - hops))

    def ring(d):
        if d:
            ups[d].wait_recv()
        send_up(d + 2, 2)
        if d:
            dns[d].wait_recv()
        if d < 6:
            send_dn(d + 2, 2)
        send_up(d + 1, 1)
        send_dn(d + 1, 1)

    ring(0)
    for cp in nin:
        cp.wait_recv()
    nsib = go(N_SIB, nkv.at[c], nkv.at[c], dev(core=oc))
    odd = lax.rem(z, 2) == 1
    upper = jnp.logical_not(odd) & (z > 0)
    lower = odd & (z < NZ - 1)

    for slot in (1, 2, 3):
        cq[slot].wait_recv()
    r = acc[2] + dot(tk(1), wq[1]) + dot(tk(2), wq[2]) + dot(tk(3), wq[3])
    for h in range(HEADS):
        proj[h] = r[:, 128 * h:128 * h + 128].astype(BF).reshape(8, 64, HD)
    ring(2)
    for h in range(HEADS):
        fqs[h] = rows(h, fb[h])
        nqs[h] = rows(h, nbk[h])
    down = [rc(N_QD + j, nqs.at[lax.rem(y + j, 4)], ncq.at[y], dev(dy=j, dz=NZ - 1)) for j in (0, 1, 2, 3)]

    @pl.when(upper)
    def _():
        for j in (0, 1, 3, 2):
            down[j].start()

    qin = []
    for j in (1, 3, 2):
        t = lax.rem(y + j, 4)
        qin.append(go(N_Q + j - 1, nqs.at[t], nq.at[y], dev(dy=j)))
    nq[y] = nqs[y]
    fqin = []
    for j in (0, 1, 2, 3):
        t = lax.rem(y + j, 4)
        for core in (c, oc):
            if j or core is oc:
                fqin.append(go(F_Q + len(fqin), fqs.at[t], fqc.at[me], dev(dy=j, core=core)))
    fqc[me] = fqs[y]

    def pack(lse):
        t = lse.T[0:16]
        a = t.astype(BF).astype(F32)
        b = (t - a).astype(BF).astype(F32)
        row = lax.broadcasted_iota(jnp.int32, (16, 128), 0)
        return jnp.where(row == 0, a, jnp.where(row == 1, b, t - a - b)).astype(BF)

    qi = lax.broadcasted_iota(jnp.int32, (128, 128), 0)
    ki = lax.broadcasted_iota(jnp.int32, (128, 128), 1)
    causal = ki <= qi

    def local(h, i):
        n = 128 * i
        q = span(h, n, n + 128)
        s1 = jnp.where(causal, qk(q, span(4 + h, n, n + 128)), NEG)
        top = jnp.max(s1, axis=1, keepdims=True)
        if i:
            s0 = qk(q, span(4 + h, 0, n))
            top = jnp.maximum(top, jnp.max(s0, axis=1, keepdims=True))
        p1 = jnp.exp(s1 - top)
        tot = jnp.sum(p1, axis=1, keepdims=True)
        o = pv(p1, span(8 + h, n, n + 128))
        if i:
            p0 = jnp.exp(s0 - top)
            tot = tot + jnp.sum(p0, axis=1, keepdims=True)
            o = o + pv(p0, span(8 + h, 0, n))
        lo[h, i] = o / tot
        ll[h, i] = lanes(top + jnp.log(tot))

    for h in (0, 1):
        for i in range(4):
            local(h, i)
    ring(4)

    def finish(to, i, pairs, tops):
        top = tops[0]
        for t in tops[1:]:
            top = jnp.maximum(top, t)
        tot, o = 0.0, 0.0
        for sc, v in pairs:
            p = jnp.exp(sc - top)
            tot = tot + jnp.sum(p, axis=1, keepdims=True)
            o = o + pv(p, v)
        to[i, 0:128] = (o / tot).astype(BF)
        to[i, 128:144] = pack(lanes(top + jnp.log(tot)))

    def near_plane(i):
        q = nq[i]
        m = 128 * (i + 1)
        sa = qk(q, nkv[c, 0, 0:i + 1].reshape(m, HD))
        sb = qk(q, nkv[oc, 0, 0:i + 1].reshape(m, HD))
        kk = lax.broadcasted_iota(jnp.int32, (128, m), 1)
        qq = lax.broadcasted_iota(jnp.int32, (128, m), 0) + 128 * i
        sa = jnp.where(kk <= qq, sa, NEG)
        sb = jnp.where(kk < 128 * (i + c), sb, NEG)
        finish(nos, i, [(sa, nkv[c, 1, 0:i + 1].reshape(m, HD)), (sb, nkv[oc, 1, 0:i + 1].reshape(m, HD))],
               [jnp.max(sa, axis=1, keepdims=True), jnp.max(sb, axis=1, keepdims=True)])

    nsib.wait_recv()
    for cp in qin:
        cp.wait_recv()
    for i in range(4):
        near_plane(i)
    nback = []
    for j in (1, 3, 2):
        nback.append(go(N_O + j - 1, nos.at[lax.rem(y + j, 4)], nor.at[y], dev(dy=j)))
    nor[y] = nos[y]

    back = [rc(N_OC + j, cos.at[lax.rem(y + j, 4)], cor.at[y], dev(dy=j, dz=1)) for j in (0, 1, 2, 3)]

    @pl.when(lower)
    def _():
        for j in (0, 1, 3, 2):
            down[j].wait_recv()
        for i in range(4):
            q = ncq[i]
            ss = [qk(q, nkv[d, 0].reshape(512, HD)) for d in (0, 1)]
            finish(cos, i, [(ss[d], nkv[d, 1].reshape(512, HD)) for d in (0, 1)],
                   [jnp.max(t, axis=1, keepdims=True) for t in ss])
        for j in (0, 1, 3, 2):
            back[j].start()

    @pl.when(jnp.logical_not(upper))
    def _():
        for h in range(HEADS):
            cor[h, 0:128] = jnp.zeros((128, HD), BF)
            cor[h, 128:144] = jnp.full((16, HD), NEG, BF)

    ring(6)
    for h in (2, 3):
        for i in range(4):
            local(h, i)
    for cp in fqin:
        cp.wait_recv()
    for d in (1, 3, 5, 7, 8):
        ups[d].wait_recv()
        if d < 8:
            dns[d].wait_recv()

    sf = qk(fqc[holder], kvf[:, 0].reshape(1024, HD))
    kk = lax.broadcasted_iota(jnp.int32, (128, 1024), 1)
    qq = lax.broadcasted_iota(jnp.int32, (128, 1024), 0)
    dist = lax.shift_right_logical(kk, 6)
    seen = (dist <= z) & ((dist > 0) | (kk + 64 * c <= qq))
    sf = jnp.where(seen, sf, NEG)
    top = jnp.max(sf, axis=1, keepdims=True)
    pf = jnp.exp(sf - top)
    tot = jnp.sum(pf, axis=1, keepdims=True)
    fos[0:128] = (pv(pf, kvf[:, 1].reshape(1024, HD)) / tot).astype(BF)
    fos[128:144] = pack(lanes(top + jnp.log(tot)))
    fback = []
    n = 0
    for dy in (1, 3, 2, 0):
        for core in (c, oc):
            if dy == 0 and core is c:
                continue
            fback.append(go(F_O + n, fos, fo.at[y, c], dev(dy=dy, core=core)))
            n += 1
    fo[y, c] = fos[...]

    def spread(tile):
        t = tile.astype(F32)
        return jnp.broadcast_to(t[0:1] + t[1:2] + t[2:3], (128, 128)).T

    for cp in nback:
        cp.wait_recv()

    @pl.when(upper)
    def _():
        for j in (0, 1, 3, 2):
            back[j].wait_recv()

    for h in range(HEADS):
        plane_l = spread(nor[h, 128:144])
        cross_l = spread(cor[h, 128:144])
        near_l = jnp.maximum(plane_l, cross_l)
        wp = jnp.exp(plane_l - near_l)
        wc = jnp.exp(cross_l - near_l)
        near_o = wp * nor[h, 0:128].astype(F32) + wc * cor[h, 0:128].astype(F32)
        near_w = wp + wc
        near_at = jnp.full((128, 128), nbk[h], jnp.int32)
        for b in range(4):
            ln = jnp.where(near_at == b, near_l, NEG)
            l0 = ll[h, b]
            best = jnp.maximum(l0, ln)
            w0 = jnp.exp(l0 - best)
            wn = jnp.exp(ln - best)
            lo[h, b] = w0 * lo[h, b] + wn * near_o
            nw[h, b] = w0 + wn * near_w
            ll[h, b] = best
    for cp in fback:
        cp.wait_recv()
    for h in range(HEADS):
        far_l = [spread(fo[h, d, 128:144]) for d in (0, 1)]
        far_o = [fo[h, d, 0:128].astype(F32) for d in (0, 1)]
        far_at = jnp.full((128, 128), foff[h], jnp.int32)
        for b in range(4):
            is_far = far_at == lax.rem(seq, 8) * 4 + b
            lf = [jnp.where(is_far, v, NEG) for v in far_l]
            l0 = ll[h, b]
            best = jnp.maximum(l0, jnp.maximum(lf[0], lf[1]))
            w0 = jnp.exp(l0 - best)
            wf = [jnp.exp(v - best) for v in lf]
            num = w0 * lo[h, b] + wf[0] * far_o[0] + wf[1] * far_o[1]
            out[b * 128:b * 128 + 128, h * 128:h * 128 + 128] = (num / (w0 * nw[h, b] + wf[0] + wf[1])).astype(BF)

    for cp in pend:
        cp.wait_send()

    @pl.when(upper)
    def _():
        for cp in down:
            cp.wait_send()

    @pl.when(lower)
    def _():
        for cp in back:
            cp.wait_send()


def body(tokens, qkv_weight, near_offset, far_offset):
    vm = pltpu.VMEM
    mixed = pl.pallas_call(
        kernel,
        out_shape=jax.ShapeDtypeStruct((512, 512), BF),
        in_specs=[pl.BlockSpec(memory_space=pl.ANY)] * 4,
        out_specs=pl.BlockSpec(memory_space=pltpu.VMEM),
        scratch_shapes=[
            vm((4, 512, 512), BF),
            vm((4, 512, 512), BF),
            vm((4, 512, 512), BF),
            vm((4, 512, 512), BF),
            vm((3, 512, 512), F32),
            vm((12, 8, 64, 128), BF),
            vm((2, 4, 2, 64, 128), BF),
            vm((4, 128, 128), BF),
            vm((8, 2, 64, 128), BF),
            vm((8, 128, 128), BF),
            vm((16, 2, 64, 128), BF),
            vm((4, 128, 128), BF),
            vm((4, 2, 128, 128), BF),
            vm((4, 128, 128), BF),
            vm((2, 2, 4, 128, 128), BF),
            vm((4, 128, 128), BF),
            vm((4, 144, 128), BF),
            vm((4, 144, 128), BF),
            vm((4, 144, 128), BF),
            vm((4, 144, 128), BF),
            vm((144, 128), BF),
            vm((4, 2, 144, 128), BF),
            vm((4, 4, 128, 128), F32),
            vm((4, 4, 128, 128), F32),
            vm((4, 4, 128, 128), F32),
            pltpu.SMEM((4,), jnp.int32),
            pltpu.SMEM((4,), jnp.int32),
            pltpu.SemaphoreType.DMA((N_SEM,)),
            pltpu.SemaphoreType.DMA((N_SEM,)),
            pltpu.SemaphoreType.DMA((9,)),
        ],
        compiler_params=pltpu.CompilerParams(
            collective_id=0, has_side_effects=True, vmem_limit_bytes=60 * 1024 * 1024),
    )(tokens[0], qkv_weight, near_offset, far_offset)
    return mixed[None]


def solution(mesh):
    in_specs = (P("fsdp", "seq", None), P("fsdp", None), P(), P())
    out_specs = P("fsdp", "seq", None)
    return jax.shard_map(body, mesh=mesh, in_specs=in_specs, out_specs=out_specs, check_vma=False)
```

```python
import jax
import jax.numpy as jnp
from jax import lax
from jax.experimental import pallas as pl
from jax.experimental.pallas import tpu as pltpu
from jax.sharding import PartitionSpec as P

HEADS = 4
HD = 128
NZ = 16
SCALE = HD ** (-0.5)
NEG = -1e30
BF = jnp.bfloat16
F32 = jnp.float32

X_W, X_Q, SIDE, C_X, C_SIDE, C_Q = 0, 6, 9, 21, 25, 37
F_KV, F_Q, N_Q, N_KV, N_SIB = 40, 47, 54, 57, 60
R_UP, R_DN, N_O, F_O, N_QD, N_OC = 61, 69, 76, 79, 86, 90
N_SEM = 94


def qk(q, k):
    return lax.dot_general(q, k, (((1,), (1,)), ((), ())), preferred_element_type=F32) * SCALE


def pv(p, v):
    return jnp.dot(p.astype(BF), v, preferred_element_type=F32)


def lanes(column):
    return jnp.broadcast_to(column, (128, 128))


def kernel(tok, wgt, noff_h, foff_h, out, wk, wv, wq, tokv, acc, proj, fkvs, fqs, fkvc, fqc, kvf,
           nqs, nks, nq, nkv, ncq, cos, cor, nos, nor, fos, fo, lo, ll, nw,
           noff, foff, ssem, rsem, lsem):
    seq = lax.axis_index("seq")
    x = lax.axis_index("fsdp")
    z = lax.div(seq, 8)
    y = lax.rem(lax.div(seq, 2), 4)
    c = lax.rem(seq, 2)
    oc = 1 - c

    def dev(dx=0, dy=0, dz=0, core=c):
        return (lax.rem(z + dz, NZ) * 8 + lax.rem(y + dy, 4) * 2 + core, lax.rem(x + dx, 4))

    pend = []

    def rc(k, src, dst, to):
        return pltpu.make_async_remote_copy(
            src_ref=src, dst_ref=dst, send_sem=ssem.at[k], recv_sem=rsem.at[k],
            device_id=to, device_id_type=pl.DeviceIdType.MESH)

    def go(k, src, dst, to):
        cp = rc(k, src, dst, to)
        cp.start()
        pend.append(cp)
        return cp

    loads = [pltpu.make_async_copy(tok.at[:, pl.ds(512 * k, 512)], tokv.at[k], lsem.at[k]) for k in range(4)]
    loads.append(pltpu.make_async_copy(wgt.at[:, pl.ds(512, 512)], wk.at[0], lsem.at[4]))
    loads.append(pltpu.make_async_copy(wgt.at[:, pl.ds(1024, 512)], wv.at[0], lsem.at[5]))
    loads.append(pltpu.make_async_copy(wgt.at[:, pl.ds(0, 512)], wq.at[0], lsem.at[6]))
    loads.append(pltpu.make_async_copy(noff_h, noff, lsem.at[7]))
    loads.append(pltpu.make_async_copy(foff_h, foff, lsem.at[8]))
    for ld in loads:
        ld.start()
    barrier = pltpu.get_barrier_semaphore()
    peers = [dev(dx=d) for d in (1, 2, 3)] + [dev(dz=d) for d in (1, 2, NZ - 2, NZ - 1)] + [dev(core=oc)]
    for dy in (1, 2, 3):
        peers += [dev(dy=dy), dev(dy=dy, core=oc), dev(dy=dy, dz=1), dev(dy=dy, dz=NZ - 1)]
    for peer in peers:
        pl.semaphore_signal(barrier, inc=1, device_id=peer, device_id_type=pl.DeviceIdType.MESH)
    pl.semaphore_wait(barrier, len(peers))

    place = (y, lax.rem(z, 4))

    def strip(pos, core=c):
        return pl.ds(pl.multiple_of(128 * pos + 64 * core, 64), 64)

    kv_w = (wk, wv)
    xw, xq = {}, {}

    def x_send(slot, dx):
        for n in (0, 1):
            r = strip(place[n])
            xw[n, slot] = go(X_W + n * 3 + slot - 1, wgt.at[r, pl.ds(512 + 512 * n, 512)],
                             kv_w[n].at[slot, r], dev(dx=dx))

    x_send(1, 3)
    x_send(2, 1)
    for ld in loads:
        ld.wait()

    def tk(slot):
        return tokv[lax.rem(x + (0, 1, 3, 2)[slot], 4)]

    def dot(a, b):
        return jnp.dot(a, b, preferred_element_type=F32)

    for n in (0, 1):
        acc[n] = dot(tk(0), kv_w[n][0])
    x_send(3, 2)

    def side_dev(n, j):
        if n == 0:
            return dev(dy=j)
        return dev(dz=(1, 2 + (NZ - 4) * c, NZ - 1)[j - 1])

    groups = (pl.ds(1, 2), pl.ds(3, 1))
    sw, cx, cs = {}, {}, {}
    for g in (0, 1):
        for n in (0, 1):
            for slot in ((1, 2), (3,))[g]:
                xw[n, slot].wait_recv()
            part = kv_w[n].at[groups[g], strip(place[n])]
            for j in (1, 2, 3):
                sw[g, n, j] = go(SIDE + g * 6 + n * 3 + j - 1, part, part, side_dev(n, j))
            cx[g, n] = go(C_X + g * 2 + n, part, part, dev(core=oc))

    half = pl.ds(pl.multiple_of(256 * c, 256), 256)
    for slot, dx in ((1, 3), (2, 1), (3, 2)):
        xq[slot] = go(X_Q + slot - 1, wgt.at[half, pl.ds(0, 512)], wq.at[slot, half], dev(dx=dx))

    def arrived(n, j):
        return strip(lax.rem(place[n] + 4 - j, 4))

    def side_arrivals(g):
        for j in (1, 3, 2):
            for n in (0, 1):
                sw[g, n, j].wait_recv()
                part = kv_w[n].at[groups[g], arrived(n, j)]
                cs[g, n, j] = go(C_SIDE + g * 6 + n * 3 + j - 1, part, part, dev(core=oc))

    acc[2] = dot(tk(0), wq[0])
    side_arrivals(0)
    side_arrivals(1)
    for n in (0, 1):
        cx[0, n].wait_recv()
        for j in (1, 3, 2):
            cs[0, n, j].wait_recv()
        acc[n] += dot(tk(1), kv_w[n][1]) + dot(tk(2), kv_w[n][2])
    for n in (0, 1):
        cx[1, n].wait_recv()
        for j in (1, 3, 2):
            cs[1, n, j].wait_recv()
        r = acc[n] + dot(tk(3), kv_w[n][3])
        for h in range(HEADS):
            proj[4 + 4 * n + h] = r[:, 128 * h:128 * h + 128].astype(BF).reshape(8, 64, HD)

    def rows(j, b):
        return proj[j, pl.ds(2 * b, 2)].reshape(128, HD)

    def span(j, n, m):
        return proj[j, n // 64:m // 64].reshape(m - n, HD)

    fb = [lax.rem(foff[h], 4) for h in range(HEADS)]
    nbk = [noff[h] for h in range(HEADS)]
    for h in range(HEADS):
        for d in (0, 1):
            fkvs[d, h, 0] = proj[4 + h, 2 * fb[h] + d]
            fkvs[d, h, 1] = proj[8 + h, 2 * fb[h] + d]
    me = 2 * y + c
    fin = []
    for j in (0, 1, 2, 3):
        t = lax.rem(y + j, 4)
        for core in (c, oc):
            if j or core is oc:
                fin.append(go(F_KV + len(fin), fkvs.at[core, t], fkvc.at[me], dev(dy=j, core=core)))
    fkvc[me] = fkvs[c, y]
    for h in range(HEADS):
        nks[h, 0] = rows(4 + h, nbk[h])
        nks[h, 1] = rows(8 + h, nbk[h])
    nin = []
    for j in (1, 3, 2):
        t = lax.rem(y + j, 4)
        nin.append(go(N_KV + j - 1, nks.at[t], nkv.at[c, :, y], dev(dy=j)))
    nkv[c, 0, y] = nks[y, 0]
    nkv[c, 1, y] = nks[y, 1]

    cq = {}
    for slot in (1, 2, 3):
        xq[slot].wait_recv()
        cq[slot] = go(C_Q + slot - 1, wq.at[slot, half], wq.at[slot, half], dev(core=oc))

    for cp in fin:
        cp.wait_recv()
    holder = lax.div(foff[y], 4)
    kvf[0] = fkvc[holder]
    ups, dns = {}, {}

    def send_up(d, hops):
        ups[d] = go(R_UP + d - 1, kvf.at[d - hops], kvf.at[d], dev(dz=hops))

    def send_dn(d, hops):
        src = 0 if d == hops else 16 - d + hops
        dns[d] = go(R_DN + d - 1, kvf.at[src], kvf.at[16 - d], dev(dz=NZ - hops))

    def ring(d):
        if d:
            ups[d].wait_recv()
        send_up(d + 2, 2)
        if d:
            dns[d].wait_recv()
        if d < 6:
            send_dn(d + 2, 2)
        send_up(d + 1, 1)
        send_dn(d + 1, 1)

    ring(0)
    for cp in nin:
        cp.wait_recv()
    nsib = go(N_SIB, nkv.at[c], nkv.at[c], dev(core=oc))
    odd = lax.rem(z, 2) == 1
    upper = jnp.logical_not(odd) & (z > 0)
    lower = odd & (z < NZ - 1)

    for slot in (1, 2, 3):
        cq[slot].wait_recv()
    r = acc[2] + dot(tk(1), wq[1]) + dot(tk(2), wq[2]) + dot(tk(3), wq[3])
    for h in range(HEADS):
        proj[h] = r[:, 128 * h:128 * h + 128].astype(BF).reshape(8, 64, HD)
    ring(2)
    for h in range(HEADS):
        fqs[h] = rows(h, fb[h])
        nqs[h] = rows(h, nbk[h])
    down = [rc(N_QD + j, nqs.at[lax.rem(y + j, 4)], ncq.at[y], dev(dy=j, dz=NZ - 1)) for j in (0, 1, 2, 3)]

    @pl.when(upper)
    def _():
        for j in (0, 1, 3, 2):
            down[j].start()

    qin = []
    for j in (1, 3, 2):
        t = lax.rem(y + j, 4)
        qin.append(go(N_Q + j - 1, nqs.at[t], nq.at[y], dev(dy=j)))
    nq[y] = nqs[y]
    fqin = []
    for j in (0, 1, 2, 3):
        t = lax.rem(y + j, 4)
        for core in (c, oc):
            if j or core is oc:
                fqin.append(go(F_Q + len(fqin), fqs.at[t], fqc.at[me], dev(dy=j, core=core)))
    fqc[me] = fqs[y]

    def pack(lse):
        t = lse.T[0:16]
        a = t.astype(BF).astype(F32)
        b = (t - a).astype(BF).astype(F32)
        row = lax.broadcasted_iota(jnp.int32, (16, 128), 0)
        return jnp.where(row == 0, a, jnp.where(row == 1, b, t - a - b)).astype(BF)

    qi = lax.broadcasted_iota(jnp.int32, (128, 128), 0)
    ki = lax.broadcasted_iota(jnp.int32, (128, 128), 1)
    causal = ki <= qi

    def local(h, i):
        n = 128 * i
        q = span(h, n, n + 128)
        s1 = jnp.where(causal, qk(q, span(4 + h, n, n + 128)), NEG)
        top = jnp.max(s1, axis=1, keepdims=True)
        if i:
            s0 = qk(q, span(4 + h, 0, n))
            top = jnp.maximum(top, jnp.max(s0, axis=1, keepdims=True))
        p1 = jnp.exp(s1 - top)
        tot = jnp.sum(p1, axis=1, keepdims=True)
        o = pv(p1, span(8 + h, n, n + 128))
        if i:
            p0 = jnp.exp(s0 - top)
            tot = tot + jnp.sum(p0, axis=1, keepdims=True)
            o = o + pv(p0, span(8 + h, 0, n))
        lo[h, i] = o / tot
        ll[h, i] = lanes(top + jnp.log(tot))

    for h in (0, 1):
        for i in range(4):
            local(h, i)
    ring(4)

    def finish(to, i, pairs, tops):
        top = tops[0]
        for t in tops[1:]:
            top = jnp.maximum(top, t)
        tot, o = 0.0, 0.0
        for sc, v in pairs:
            p = jnp.exp(sc - top)
            tot = tot + jnp.sum(p, axis=1, keepdims=True)
            o = o + pv(p, v)
        to[i, 0:128] = (o / tot).astype(BF)
        to[i, 128:144] = pack(lanes(top + jnp.log(tot)))

    def near_plane(i):
        q = nq[i]
        m = 128 * (i + 1)
        sa = qk(q, nkv[c, 0, 0:i + 1].reshape(m, HD))
        sb = qk(q, nkv[oc, 0, 0:i + 1].reshape(m, HD))
        kk = lax.broadcasted_iota(jnp.int32, (128, m), 1)
        qq = lax.broadcasted_iota(jnp.int32, (128, m), 0) + 128 * i
        sa = jnp.where(kk <= qq, sa, NEG)
        sb = jnp.where(kk < 128 * (i + c), sb, NEG)
        finish(nos, i, [(sa, nkv[c, 1, 0:i + 1].reshape(m, HD)), (sb, nkv[oc, 1, 0:i + 1].reshape(m, HD))],
               [jnp.max(sa, axis=1, keepdims=True), jnp.max(sb, axis=1, keepdims=True)])

    nsib.wait_recv()
    for cp in qin:
        cp.wait_recv()
    for i in range(4):
        near_plane(i)
    nback = []
    for j in (1, 3, 2):
        nback.append(go(N_O + j - 1, nos.at[lax.rem(y + j, 4)], nor.at[y], dev(dy=j)))
    nor[y] = nos[y]

    back = [rc(N_OC + j, cos.at[lax.rem(y + j, 4)], cor.at[y], dev(dy=j, dz=1)) for j in (0, 1, 2, 3)]

    @pl.when(lower)
    def _():
        for j in (0, 1, 3, 2):
            down[j].wait_recv()
        for i in range(4):
            q = ncq[i]
            ss = [qk(q, nkv[d, 0].reshape(512, HD)) for d in (0, 1)]
            finish(cos, i, [(ss[d], nkv[d, 1].reshape(512, HD)) for d in (0, 1)],
                   [jnp.max(t, axis=1, keepdims=True) for t in ss])
        for j in (0, 1, 3, 2):
            back[j].start()

    @pl.when(jnp.logical_not(upper))
    def _():
        for h in range(HEADS):
            cor[h, 0:128] = jnp.zeros((128, HD), BF)
            cor[h, 128:144] = jnp.full((16, HD), NEG, BF)

    ring(6)
    for h in (2, 3):
        for i in range(4):
            local(h, i)
    for cp in fqin:
        cp.wait_recv()
    for d in (1, 3, 5):
        ups[d].wait_recv()
        dns[d].wait_recv()

    fq = fqc[holder]
    ranges = ((0, 7), (10, 16), (7, 10))

    def far_scores(a, b):
        m = 64 * (b - a)
        kk = lax.broadcasted_iota(jnp.int32, (128, m), 1) + 64 * a
        qq = lax.broadcasted_iota(jnp.int32, (128, m), 0)
        seen = lax.shift_right_logical(kk, 6) <= z
        if a == 0:
            seen = seen & ((kk >= 64) | (kk + 64 * c <= qq))
        return jnp.where(seen, qk(fq, kvf[a:b, 0].reshape(m, HD)), NEG)

    def far_part(top, a, b, sc):
        p = jnp.exp(sc - top)
        return jnp.sum(p, axis=1, keepdims=True), pv(p, kvf[a:b, 1].reshape(64 * (b - a), HD))

    early = [far_scores(a, b) for a, b in ranges[:2]]
    top0 = jnp.maximum(jnp.max(early[0], axis=1, keepdims=True), jnp.max(early[1], axis=1, keepdims=True))
    parts = [far_part(top0, a, b, sc) for (a, b), sc in zip(ranges[:2], early)]
    for cp in (ups[7], dns[7], ups[8]):
        cp.wait_recv()
    late = far_scores(*ranges[2])
    top = jnp.maximum(top0, jnp.max(late, axis=1, keepdims=True))
    w = jnp.exp(top0 - top)
    tl, ol = far_part(top, *ranges[2], late)
    tot = w * (parts[0][0] + parts[1][0]) + tl
    fos[0:128] = ((w * (parts[0][1] + parts[1][1]) + ol) / tot).astype(BF)
    fos[128:144] = pack(lanes(top + jnp.log(tot)))
    fback = [[], [], [], []]
    n = 0
    for dy in (2, 1, 3, 0):
        for core in (c, oc):
            if dy == 0 and core is c:
                continue
            fback[dy].append(go(F_O + n, fos, fo.at[y, c], dev(dy=dy, core=core)))
            n += 1
    fo[y, c] = fos[...]

    def spread(tile):
        t = tile.astype(F32)
        return jnp.broadcast_to(t[0:1] + t[1:2] + t[2:3], (128, 128)).T

    for cp in nback:
        cp.wait_recv()

    @pl.when(upper)
    def _():
        for j in (0, 1, 3, 2):
            back[j].wait_recv()

    for h in range(HEADS):
        plane_l = spread(nor[h, 128:144])
        cross_l = spread(cor[h, 128:144])
        near_l = jnp.maximum(plane_l, cross_l)
        wp = jnp.exp(plane_l - near_l)
        wc = jnp.exp(cross_l - near_l)
        near_o = wp * nor[h, 0:128].astype(F32) + wc * cor[h, 0:128].astype(F32)
        near_w = wp + wc
        near_at = jnp.full((128, 128), nbk[h], jnp.int32)
        for b in range(4):
            ln = jnp.where(near_at == b, near_l, NEG)
            l0 = ll[h, b]
            best = jnp.maximum(l0, ln)
            w0 = jnp.exp(l0 - best)
            wn = jnp.exp(ln - best)
            lo[h, b] = w0 * lo[h, b] + wn * near_o
            nw[h, b] = w0 + wn * near_w
            ll[h, b] = best
    for dy in (0, 1, 3, 2):
        for cp in fback[dy]:
            cp.wait_recv()
        h = lax.rem(y + 4 - dy, 4)
        far_l = [spread(fo[h, d, 128:144]) for d in (0, 1)]
        far_o = [fo[h, d, 0:128].astype(F32) for d in (0, 1)]
        far_at = jnp.full((128, 128), foff[h], jnp.int32)
        for b in range(4):
            is_far = far_at == lax.rem(seq, 8) * 4 + b
            lf = [jnp.where(is_far, v, NEG) for v in far_l]
            l0 = ll[h, b]
            best = jnp.maximum(l0, jnp.maximum(lf[0], lf[1]))
            w0 = jnp.exp(l0 - best)
            wf = [jnp.exp(v - best) for v in lf]
            num = w0 * lo[h, b] + wf[0] * far_o[0] + wf[1] * far_o[1]
            out[b * 128:b * 128 + 128, pl.ds(pl.multiple_of(h * 128, 128), 128)] = (
                num / (w0 * nw[h, b] + wf[0] + wf[1])).astype(BF)

    for cp in pend:
        cp.wait_send()

    @pl.when(upper)
    def _():
        for cp in down:
            cp.wait_send()

    @pl.when(lower)
    def _():
        for cp in back:
            cp.wait_send()


def body(tokens, qkv_weight, near_offset, far_offset):
    vm = pltpu.VMEM
    mixed = pl.pallas_call(
        kernel,
        out_shape=jax.ShapeDtypeStruct((512, 512), BF),
        in_specs=[pl.BlockSpec(memory_space=pl.ANY)] * 4,
        out_specs=pl.BlockSpec(memory_space=pltpu.VMEM),
        scratch_shapes=[
            vm((4, 512, 512), BF),
            vm((4, 512, 512), BF),
            vm((4, 512, 512), BF),
            vm((4, 512, 512), BF),
            vm((3, 512, 512), F32),
            vm((12, 8, 64, 128), BF),
            vm((2, 4, 2, 64, 128), BF),
            vm((4, 128, 128), BF),
            vm((8, 2, 64, 128), BF),
            vm((8, 128, 128), BF),
            vm((16, 2, 64, 128), BF),
            vm((4, 128, 128), BF),
            vm((4, 2, 128, 128), BF),
            vm((4, 128, 128), BF),
            vm((2, 2, 4, 128, 128), BF),
            vm((4, 128, 128), BF),
            vm((4, 144, 128), BF),
            vm((4, 144, 128), BF),
            vm((4, 144, 128), BF),
            vm((4, 144, 128), BF),
            vm((144, 128), BF),
            vm((4, 2, 144, 128), BF),
            vm((4, 4, 128, 128), F32),
            vm((4, 4, 128, 128), F32),
            vm((4, 4, 128, 128), F32),
            pltpu.SMEM((4,), jnp.int32),
            pltpu.SMEM((4,), jnp.int32),
            pltpu.SemaphoreType.DMA((N_SEM,)),
            pltpu.SemaphoreType.DMA((N_SEM,)),
            pltpu.SemaphoreType.DMA((9,)),
        ],
        compiler_params=pltpu.CompilerParams(
            collective_id=0, has_side_effects=True, vmem_limit_bytes=60 * 1024 * 1024),
    )(tokens[0], qkv_weight, near_offset, far_offset)
    return mixed[None]


def solution(mesh):
    in_specs = (P("fsdp", "seq", None), P("fsdp", None), P(), P())
    out_specs = P("fsdp", "seq", None)
    return jax.shard_map(body, mesh=mesh, in_specs=in_specs, out_specs=out_specs, check_vma=False)
```

```python
import jax
import jax.numpy as jnp
from jax import lax
from jax.experimental import pallas as pl
from jax.experimental.pallas import tpu as pltpu
from jax.sharding import PartitionSpec as P

HEADS = 4
HD = 128
NZ = 16
SCALE = HD ** (-0.5)
NEG = -1e30
BF = jnp.bfloat16
F32 = jnp.float32

X_W, X_Q, SIDE, C_X, C_SIDE, C_Q = 0, 6, 9, 21, 25, 37
F_KV, F_Q, N_Q, N_KV, N_SIB = 40, 47, 54, 57, 60
R_UP, R_DN, N_O, F_O, N_QD, N_OC = 61, 69, 76, 79, 86, 90
N_SEM = 94


def qk(q, k):
    return lax.dot_general(q, k, (((1,), (1,)), ((), ())), preferred_element_type=F32) * SCALE


def pv(p, v):
    return jnp.dot(p.astype(BF), v, preferred_element_type=F32)


def lanes(column):
    return jnp.broadcast_to(column, (128, 128))


def kernel(tok, wgt, noff_h, foff_h, out, wk, wv, wq, tokv, acc, proj, fkvs, fqs, fkvc, fqc, kvf,
           nqs, nks, nq, nkv, ncq, cos, cor, nos, nor, fos, fo, lo, ll, nw,
           noff, foff, ssem, rsem, lsem):
    seq = lax.axis_index("seq")
    x = lax.axis_index("fsdp")
    z = lax.div(seq, 8)
    y = lax.rem(lax.div(seq, 2), 4)
    c = lax.rem(seq, 2)
    oc = 1 - c

    def dev(dx=0, dy=0, dz=0, core=c):
        return (lax.rem(z + dz, NZ) * 8 + lax.rem(y + dy, 4) * 2 + core, lax.rem(x + dx, 4))

    pend = []

    def rc(k, src, dst, to):
        return pltpu.make_async_remote_copy(
            src_ref=src, dst_ref=dst, send_sem=ssem.at[k], recv_sem=rsem.at[k],
            device_id=to, device_id_type=pl.DeviceIdType.MESH)

    def go(k, src, dst, to):
        cp = rc(k, src, dst, to)
        cp.start()
        pend.append(cp)
        return cp

    loads = [pltpu.make_async_copy(tok.at[:, pl.ds(512 * k, 512)], tokv.at[k], lsem.at[k]) for k in range(4)]
    loads.append(pltpu.make_async_copy(wgt.at[:, pl.ds(512, 512)], wk.at[0], lsem.at[4]))
    loads.append(pltpu.make_async_copy(wgt.at[:, pl.ds(1024, 512)], wv.at[0], lsem.at[5]))
    loads.append(pltpu.make_async_copy(wgt.at[:, pl.ds(0, 512)], wq.at[0], lsem.at[6]))
    loads.append(pltpu.make_async_copy(noff_h, noff, lsem.at[7]))
    loads.append(pltpu.make_async_copy(foff_h, foff, lsem.at[8]))
    for ld in loads:
        ld.start()
    kvf[...] = jnp.zeros_like(kvf)
    barrier = pltpu.get_barrier_semaphore()
    peers = [dev(dx=d) for d in (1, 2, 3)] + [dev(dz=d) for d in (1, 2, NZ - 2, NZ - 1)] + [dev(core=oc)]
    for dy in (1, 2, 3):
        peers += [dev(dy=dy), dev(dy=dy, core=oc), dev(dy=dy, dz=1), dev(dy=dy, dz=NZ - 1)]
    for peer in peers:
        pl.semaphore_signal(barrier, inc=1, device_id=peer, device_id_type=pl.DeviceIdType.MESH)
    pl.semaphore_wait(barrier, len(peers))

    place = (y, lax.rem(z, 4))

    def strip(pos, core=c):
        return pl.ds(pl.multiple_of(128 * pos + 64 * core, 64), 64)

    kv_w = (wk, wv)
    xw, xq = {}, {}

    def x_send(slot, dx):
        for n in (0, 1):
            r = strip(place[n])
            xw[n, slot] = go(X_W + n * 3 + slot - 1, wgt.at[r, pl.ds(512 + 512 * n, 512)],
                             kv_w[n].at[slot, r], dev(dx=dx))

    x_send(1, 3)
    x_send(2, 1)
    for ld in loads:
        ld.wait()

    def tk(slot):
        return tokv[lax.rem(x + (0, 1, 3, 2)[slot], 4)]

    def dot(a, b):
        return jnp.dot(a, b, preferred_element_type=F32)

    for n in (0, 1):
        acc[n] = dot(tk(0), kv_w[n][0])
    x_send(3, 2)

    def side_dev(n, j):
        if n == 0:
            return dev(dy=j)
        return dev(dz=(1, 2 + (NZ - 4) * c, NZ - 1)[j - 1])

    groups = (pl.ds(1, 2), pl.ds(3, 1))
    sw, cx, cs = {}, {}, {}
    for g in (0, 1):
        for n in (0, 1):
            for slot in ((1, 2), (3,))[g]:
                xw[n, slot].wait_recv()
            part = kv_w[n].at[groups[g], strip(place[n])]
            for j in (1, 2, 3):
                sw[g, n, j] = go(SIDE + g * 6 + n * 3 + j - 1, part, part, side_dev(n, j))
            cx[g, n] = go(C_X + g * 2 + n, part, part, dev(core=oc))

    half = pl.ds(pl.multiple_of(256 * c, 256), 256)
    for slot, dx in ((1, 3), (2, 1), (3, 2)):
        xq[slot] = go(X_Q + slot - 1, wgt.at[half, pl.ds(0, 512)], wq.at[slot, half], dev(dx=dx))

    def arrived(n, j):
        return strip(lax.rem(place[n] + 4 - j, 4))

    def side_arrivals(g):
        for j in (1, 3, 2):
            for n in (0, 1):
                sw[g, n, j].wait_recv()
                part = kv_w[n].at[groups[g], arrived(n, j)]
                cs[g, n, j] = go(C_SIDE + g * 6 + n * 3 + j - 1, part, part, dev(core=oc))

    acc[2] = dot(tk(0), wq[0])
    side_arrivals(0)
    side_arrivals(1)
    for n in (0, 1):
        cx[0, n].wait_recv()
        for j in (1, 3, 2):
            cs[0, n, j].wait_recv()
        acc[n] += dot(tk(1), kv_w[n][1]) + dot(tk(2), kv_w[n][2])
    for n in (0, 1):
        cx[1, n].wait_recv()
        for j in (1, 3, 2):
            cs[1, n, j].wait_recv()
        r = acc[n] + dot(tk(3), kv_w[n][3])
        for h in range(HEADS):
            proj[4 + 4 * n + h] = r[:, 128 * h:128 * h + 128].astype(BF).reshape(8, 64, HD)

    def rows(j, b):
        return proj[j, pl.ds(2 * b, 2)].reshape(128, HD)

    def span(j, n, m):
        return proj[j, n // 64:m // 64].reshape(m - n, HD)

    fb = [lax.rem(foff[h], 4) for h in range(HEADS)]
    nbk = [noff[h] for h in range(HEADS)]
    for h in range(HEADS):
        for d in (0, 1):
            fkvs[d, h, 0] = proj[4 + h, 2 * fb[h] + d]
            fkvs[d, h, 1] = proj[8 + h, 2 * fb[h] + d]
    me = 2 * y + c
    fin = []
    for j in (0, 1, 2, 3):
        t = lax.rem(y + j, 4)
        for core in (c, oc):
            if j or core is oc:
                fin.append(go(F_KV + len(fin), fkvs.at[core, t], fkvc.at[me], dev(dy=j, core=core)))
    fkvc[me] = fkvs[c, y]
    for h in range(HEADS):
        nks[h, 0] = rows(4 + h, nbk[h])
        nks[h, 1] = rows(8 + h, nbk[h])
    nin = []
    for j in (1, 3, 2):
        t = lax.rem(y + j, 4)
        nin.append(go(N_KV + j - 1, nks.at[t], nkv.at[c, :, y], dev(dy=j)))
    nkv[c, 0, y] = nks[y, 0]
    nkv[c, 1, y] = nks[y, 1]

    cq = {}
    for slot in (1, 2, 3):
        xq[slot].wait_recv()
        cq[slot] = go(C_Q + slot - 1, wq.at[slot, half], wq.at[slot, half], dev(core=oc))

    for cp in fin:
        cp.wait_recv()
    holder = lax.div(foff[y], 4)
    kvf[0] = fkvc[holder]
    ups, dns, maybe = {}, {}, []

    def start_if(cp, needed):
        maybe.append((cp, needed))

        @pl.when(needed)
        def _():
            cp.start()

    def send_up(d, hops):
        ups[d] = rc(R_UP + d - 1, kvf.at[d - hops], kvf.at[d], dev(dz=hops))
        start_if(ups[d], (z + hops < NZ) & (z + hops >= d))

    def wanted_dn(place_z, d):
        late = place_z + d >= NZ
        return late if d % 2 else late | (place_z + d <= 6)

    def send_dn(d, hops):
        src = 0 if d == hops else 16 - d + hops
        dns[d] = rc(R_DN + d - 1, kvf.at[src], kvf.at[16 - d], dev(dz=NZ - hops))
        start_if(dns[d], wanted_dn(lax.rem(z + NZ - hops, NZ), d))

    def got_up(d):
        @pl.when(z >= d)
        def _():
            ups[d].wait_recv()

    def got_dn(d):
        @pl.when(wanted_dn(z, d))
        def _():
            dns[d].wait_recv()

    def ring(d):
        if d:
            got_up(d)
        send_up(d + 2, 2)
        if d:
            got_dn(d)
        if d < 6:
            send_dn(d + 2, 2)
        send_up(d + 1, 1)
        send_dn(d + 1, 1)

    ring(0)
    for cp in nin:
        cp.wait_recv()
    nsib = go(N_SIB, nkv.at[c], nkv.at[c], dev(core=oc))
    odd = lax.rem(z, 2) == 1
    upper = jnp.logical_not(odd) & (z > 0)
    lower = odd & (z < NZ - 1)

    for slot in (1, 2, 3):
        cq[slot].wait_recv()
    r = acc[2] + dot(tk(1), wq[1]) + dot(tk(2), wq[2]) + dot(tk(3), wq[3])
    for h in range(HEADS):
        proj[h] = r[:, 128 * h:128 * h + 128].astype(BF).reshape(8, 64, HD)
    ring(2)
    for h in range(HEADS):
        fqs[h] = rows(h, fb[h])
        nqs[h] = rows(h, nbk[h])
    down = [rc(N_QD + j, nqs.at[lax.rem(y + j, 4)], ncq.at[y], dev(dy=j, dz=NZ - 1)) for j in (0, 1, 2, 3)]

    @pl.when(upper)
    def _():
        for j in (0, 1, 3, 2):
            down[j].start()

    qin = []
    for j in (1, 3, 2):
        t = lax.rem(y + j, 4)
        qin.append(go(N_Q + j - 1, nqs.at[t], nq.at[y], dev(dy=j)))
    nq[y] = nqs[y]
    fqin = []
    for j in (0, 1, 2, 3):
        t = lax.rem(y + j, 4)
        for core in (c, oc):
            if j or core is oc:
                fqin.append(go(F_Q + len(fqin), fqs.at[t], fqc.at[me], dev(dy=j, core=core)))
    fqc[me] = fqs[y]

    def pack(lse):
        t = lse.T[0:16]
        a = t.astype(BF).astype(F32)
        b = (t - a).astype(BF).astype(F32)
        row = lax.broadcasted_iota(jnp.int32, (16, 128), 0)
        return jnp.where(row == 0, a, jnp.where(row == 1, b, t - a - b)).astype(BF)

    qi = lax.broadcasted_iota(jnp.int32, (128, 128), 0)
    ki = lax.broadcasted_iota(jnp.int32, (128, 128), 1)
    causal = ki <= qi

    def local(h, i):
        n = 128 * i
        q = span(h, n, n + 128)
        s1 = jnp.where(causal, qk(q, span(4 + h, n, n + 128)), NEG)
        top = jnp.max(s1, axis=1, keepdims=True)
        if i:
            s0 = qk(q, span(4 + h, 0, n))
            top = jnp.maximum(top, jnp.max(s0, axis=1, keepdims=True))
        p1 = jnp.exp(s1 - top)
        tot = jnp.sum(p1, axis=1, keepdims=True)
        o = pv(p1, span(8 + h, n, n + 128))
        if i:
            p0 = jnp.exp(s0 - top)
            tot = tot + jnp.sum(p0, axis=1, keepdims=True)
            o = o + pv(p0, span(8 + h, 0, n))
        lo[h, i] = o / tot
        ll[h, i] = lanes(top + jnp.log(tot))

    for h in (0, 1):
        for i in range(4):
            local(h, i)
    ring(4)

    def finish(to, i, pairs, tops):
        top = tops[0]
        for t in tops[1:]:
            top = jnp.maximum(top, t)
        tot, o = 0.0, 0.0
        for sc, v in pairs:
            p = jnp.exp(sc - top)
            tot = tot + jnp.sum(p, axis=1, keepdims=True)
            o = o + pv(p, v)
        to[i, 0:128] = (o / tot).astype(BF)
        to[i, 128:144] = pack(lanes(top + jnp.log(tot)))

    def near_plane(i):
        q = nq[i]
        m = 128 * (i + 1)
        sa = qk(q, nkv[c, 0, 0:i + 1].reshape(m, HD))
        sb = qk(q, nkv[oc, 0, 0:i + 1].reshape(m, HD))
        kk = lax.broadcasted_iota(jnp.int32, (128, m), 1)
        qq = lax.broadcasted_iota(jnp.int32, (128, m), 0) + 128 * i
        sa = jnp.where(kk <= qq, sa, NEG)
        sb = jnp.where(kk < 128 * (i + c), sb, NEG)
        finish(nos, i, [(sa, nkv[c, 1, 0:i + 1].reshape(m, HD)), (sb, nkv[oc, 1, 0:i + 1].reshape(m, HD))],
               [jnp.max(sa, axis=1, keepdims=True), jnp.max(sb, axis=1, keepdims=True)])

    nsib.wait_recv()
    for cp in qin:
        cp.wait_recv()
    for i in range(4):
        near_plane(i)
    nback = []
    for j in (1, 3, 2):
        nback.append(go(N_O + j - 1, nos.at[lax.rem(y + j, 4)], nor.at[y], dev(dy=j)))
    nor[y] = nos[y]

    back = [rc(N_OC + j, cos.at[lax.rem(y + j, 4)], cor.at[y], dev(dy=j, dz=1)) for j in (0, 1, 2, 3)]

    @pl.when(lower)
    def _():
        for j in (0, 1, 3, 2):
            down[j].wait_recv()
        for i in range(4):
            q = ncq[i]
            ss = [qk(q, nkv[d, 0].reshape(512, HD)) for d in (0, 1)]
            finish(cos, i, [(ss[d], nkv[d, 1].reshape(512, HD)) for d in (0, 1)],
                   [jnp.max(t, axis=1, keepdims=True) for t in ss])
        for j in (0, 1, 3, 2):
            back[j].start()

    @pl.when(jnp.logical_not(upper))
    def _():
        for h in range(HEADS):
            cor[h, 0:128] = jnp.zeros((128, HD), BF)
            cor[h, 128:144] = jnp.full((16, HD), NEG, BF)

    ring(6)
    for h in (2, 3):
        for i in range(4):
            local(h, i)
    for cp in fqin:
        cp.wait_recv()
    for d in (1, 3, 5):
        got_up(d)
        got_dn(d)

    fq = fqc[holder]
    ranges = ((0, 7), (10, 16), (7, 10))

    def far_scores(a, b):
        m = 64 * (b - a)
        kk = lax.broadcasted_iota(jnp.int32, (128, m), 1) + 64 * a
        qq = lax.broadcasted_iota(jnp.int32, (128, m), 0)
        seen = lax.shift_right_logical(kk, 6) <= z
        if a == 0:
            seen = seen & ((kk >= 64) | (kk + 64 * c <= qq))
        return jnp.where(seen, qk(fq, kvf[a:b, 0].reshape(m, HD)), NEG)

    def far_part(top, a, b, sc):
        p = jnp.exp(sc - top)
        return jnp.sum(p, axis=1, keepdims=True), pv(p, kvf[a:b, 1].reshape(64 * (b - a), HD))

    early = [far_scores(a, b) for a, b in ranges[:2]]
    top0 = jnp.maximum(jnp.max(early[0], axis=1, keepdims=True), jnp.max(early[1], axis=1, keepdims=True))
    parts = [far_part(top0, a, b, sc) for (a, b), sc in zip(ranges[:2], early)]
    got_up(7)
    got_dn(7)
    got_up(8)
    late = far_scores(*ranges[2])
    top = jnp.maximum(top0, jnp.max(late, axis=1, keepdims=True))
    w = jnp.exp(top0 - top)
    tl, ol = far_part(top, *ranges[2], late)
    tot = w * (parts[0][0] + parts[1][0]) + tl
    fos[0:128] = ((w * (parts[0][1] + parts[1][1]) + ol) / tot).astype(BF)
    fos[128:144] = pack(lanes(top + jnp.log(tot)))
    fback = [[], [], [], []]
    n = 0
    for dy in (2, 1, 3, 0):
        for core in (c, oc):
            if dy == 0 and core is c:
                continue
            fback[dy].append(go(F_O + n, fos, fo.at[y, c], dev(dy=dy, core=core)))
            n += 1
    fo[y, c] = fos[...]

    def spread(tile):
        t = tile.astype(F32)
        return jnp.broadcast_to(t[0:1] + t[1:2] + t[2:3], (128, 128)).T

    for cp in nback:
        cp.wait_recv()

    @pl.when(upper)
    def _():
        for j in (0, 1, 3, 2):
            back[j].wait_recv()

    for h in range(HEADS):
        plane_l = spread(nor[h, 128:144])
        cross_l = spread(cor[h, 128:144])
        near_l = jnp.maximum(plane_l, cross_l)
        wp = jnp.exp(plane_l - near_l)
        wc = jnp.exp(cross_l - near_l)
        near_o = wp * nor[h, 0:128].astype(F32) + wc * cor[h, 0:128].astype(F32)
        near_w = wp + wc
        near_at = jnp.full((128, 128), nbk[h], jnp.int32)
        for b in range(4):
            ln = jnp.where(near_at == b, near_l, NEG)
            l0 = ll[h, b]
            best = jnp.maximum(l0, ln)
            w0 = jnp.exp(l0 - best)
            wn = jnp.exp(ln - best)
            lo[h, b] = w0 * lo[h, b] + wn * near_o
            nw[h, b] = w0 + wn * near_w
            ll[h, b] = best
    for dy in (0, 1, 3, 2):
        for cp in fback[dy]:
            cp.wait_recv()
        h = lax.rem(y + 4 - dy, 4)
        far_l = [spread(fo[h, d, 128:144]) for d in (0, 1)]
        far_o = [fo[h, d, 0:128].astype(F32) for d in (0, 1)]
        far_at = jnp.full((128, 128), foff[h], jnp.int32)
        for b in range(4):
            is_far = far_at == lax.rem(seq, 8) * 4 + b
            lf = [jnp.where(is_far, v, NEG) for v in far_l]
            l0 = ll[h, b]
            best = jnp.maximum(l0, jnp.maximum(lf[0], lf[1]))
            w0 = jnp.exp(l0 - best)
            wf = [jnp.exp(v - best) for v in lf]
            num = w0 * lo[h, b] + wf[0] * far_o[0] + wf[1] * far_o[1]
            out[b * 128:b * 128 + 128, pl.ds(pl.multiple_of(h * 128, 128), 128)] = (
                num / (w0 * nw[h, b] + wf[0] + wf[1])).astype(BF)

    for cp in pend:
        cp.wait_send()
    for cp, needed in maybe:
        pl.when(needed)(cp.wait_send)

    @pl.when(upper)
    def _():
        for cp in down:
            cp.wait_send()

    @pl.when(lower)
    def _():
        for cp in back:
            cp.wait_send()


def body(tokens, qkv_weight, near_offset, far_offset):
    vm = pltpu.VMEM
    mixed = pl.pallas_call(
        kernel,
        out_shape=jax.ShapeDtypeStruct((512, 512), BF),
        in_specs=[pl.BlockSpec(memory_space=pl.ANY)] * 4,
        out_specs=pl.BlockSpec(memory_space=pltpu.VMEM),
        scratch_shapes=[
            vm((4, 512, 512), BF),
            vm((4, 512, 512), BF),
            vm((4, 512, 512), BF),
            vm((4, 512, 512), BF),
            vm((3, 512, 512), F32),
            vm((12, 8, 64, 128), BF),
            vm((2, 4, 2, 64, 128), BF),
            vm((4, 128, 128), BF),
            vm((8, 2, 64, 128), BF),
            vm((8, 128, 128), BF),
            vm((16, 2, 64, 128), BF),
            vm((4, 128, 128), BF),
            vm((4, 2, 128, 128), BF),
            vm((4, 128, 128), BF),
            vm((2, 2, 4, 128, 128), BF),
            vm((4, 128, 128), BF),
            vm((4, 144, 128), BF),
            vm((4, 144, 128), BF),
            vm((4, 144, 128), BF),
            vm((4, 144, 128), BF),
            vm((144, 128), BF),
            vm((4, 2, 144, 128), BF),
            vm((4, 4, 128, 128), F32),
            vm((4, 4, 128, 128), F32),
            vm((4, 4, 128, 128), F32),
            pltpu.SMEM((4,), jnp.int32),
            pltpu.SMEM((4,), jnp.int32),
            pltpu.SemaphoreType.DMA((N_SEM,)),
            pltpu.SemaphoreType.DMA((N_SEM,)),
            pltpu.SemaphoreType.DMA((9,)),
        ],
        compiler_params=pltpu.CompilerParams(
            collective_id=0, has_side_effects=True, vmem_limit_bytes=60 * 1024 * 1024),
    )(tokens[0], qkv_weight, near_offset, far_offset)
    return mixed[None]


def solution(mesh):
    in_specs = (P("fsdp", "seq", None), P("fsdp", None), P(), P())
    out_specs = P("fsdp", "seq", None)
    return jax.shard_map(body, mesh=mesh, in_specs=in_specs, out_specs=out_specs, check_vma=False)
```

```python
import jax
import jax.numpy as jnp
from jax import lax
from jax.experimental import pallas as pl
from jax.experimental.pallas import tpu as pltpu
from jax.sharding import PartitionSpec as P

HEADS = 4
HD = 128
NZ = 16
SCALE = HD ** (-0.5)
NEG = -1e30
BF = jnp.bfloat16
F32 = jnp.float32

X_W, X_Q, SIDE, C_X, C_SIDE, C_Q = 0, 6, 9, 21, 25, 37
F_KV, F_Q, N_Q, N_KV, N_SIB = 40, 47, 54, 57, 60
R_UP, R_DN, N_O, F_O, N_QD, N_OC = 61, 69, 76, 79, 86, 90
N_SEM = 94


def qk(q, k):
    return lax.dot_general(q, k, (((1,), (1,)), ((), ())), preferred_element_type=F32) * SCALE


def pv(p, v):
    return jnp.dot(p.astype(BF), v, preferred_element_type=F32)


def lanes(column):
    return jnp.broadcast_to(column, (128, 128))


def kernel(tok, wgt, noff_h, foff_h, out, wk, wv, wq, tokv, acc, proj, fkvs, fqs, fkvc, fqc, kvf,
           nqs, nks, nq, nkv, ncq, cos, cor, nos, nor, fos, fo, lo, ll, nw,
           noff, foff, ssem, rsem, lsem):
    seq = lax.axis_index("seq")
    x = lax.axis_index("fsdp")
    z = lax.div(seq, 8)
    y = lax.rem(lax.div(seq, 2), 4)
    c = lax.rem(seq, 2)
    oc = 1 - c

    def dev(dx=0, dy=0, dz=0, core=c):
        return (lax.rem(z + dz, NZ) * 8 + lax.rem(y + dy, 4) * 2 + core, lax.rem(x + dx, 4))

    pend = []

    def rc(k, src, dst, to):
        return pltpu.make_async_remote_copy(
            src_ref=src, dst_ref=dst, send_sem=ssem.at[k], recv_sem=rsem.at[k],
            device_id=to, device_id_type=pl.DeviceIdType.MESH)

    def go(k, src, dst, to):
        cp = rc(k, src, dst, to)
        cp.start()
        pend.append(cp)
        return cp

    loads = [pltpu.make_async_copy(tok.at[:, pl.ds(512 * k, 512)], tokv.at[k], lsem.at[k]) for k in range(4)]
    loads.append(pltpu.make_async_copy(wgt.at[:, pl.ds(512, 512)], wk.at[0], lsem.at[4]))
    loads.append(pltpu.make_async_copy(wgt.at[:, pl.ds(1024, 512)], wv.at[0], lsem.at[5]))
    loads.append(pltpu.make_async_copy(wgt.at[:, pl.ds(0, 512)], wq.at[0], lsem.at[6]))
    loads.append(pltpu.make_async_copy(noff_h, noff, lsem.at[7]))
    loads.append(pltpu.make_async_copy(foff_h, foff, lsem.at[8]))
    for ld in loads:
        ld.start()
    kvf[...] = jnp.zeros_like(kvf)
    barrier = pltpu.get_barrier_semaphore()
    peers = [dev(dx=d) for d in (1, 2, 3)] + [dev(dz=d) for d in (1, 2, NZ - 2, NZ - 1)] + [dev(core=oc)]
    for dy in (1, 2, 3):
        peers += [dev(dy=dy), dev(dy=dy, core=oc), dev(dy=dy, dz=1), dev(dy=dy, dz=NZ - 1)]
    for peer in peers:
        pl.semaphore_signal(barrier, inc=1, device_id=peer, device_id_type=pl.DeviceIdType.MESH)
    pl.semaphore_wait(barrier, len(peers))

    place = (y, lax.rem(z, 4))

    def strip(pos, core=c):
        return pl.ds(pl.multiple_of(128 * pos + 64 * core, 64), 64)

    kv_w = (wk, wv)
    xw, xq = {}, {}

    def x_send(slot, dx):
        for n in (0, 1):
            r = strip(place[n])
            xw[n, slot] = go(X_W + n * 3 + slot - 1, wgt.at[r, pl.ds(512 + 512 * n, 512)],
                             kv_w[n].at[slot, r], dev(dx=dx))

    x_send(1, 3)
    x_send(2, 1)
    for ld in loads:
        ld.wait()

    def tk(slot):
        return tokv[lax.rem(x + (0, 1, 3, 2)[slot], 4)]

    def dot(a, b):
        return jnp.dot(a, b, preferred_element_type=F32)

    for n in (0, 1):
        acc[n] = dot(tk(0), kv_w[n][0])
    x_send(3, 2)

    def side_dev(n, j):
        if n == 0:
            return dev(dy=j)
        return dev(dz=(1, 2 + (NZ - 4) * c, NZ - 1)[j - 1])

    groups = (pl.ds(1, 2), pl.ds(3, 1))
    sw, cx, cs = {}, {}, {}
    for g in (0, 1):
        for n in (0, 1):
            for slot in ((1, 2), (3,))[g]:
                xw[n, slot].wait_recv()
            part = kv_w[n].at[groups[g], strip(place[n])]
            for j in (1, 2, 3):
                sw[g, n, j] = go(SIDE + g * 6 + n * 3 + j - 1, part, part, side_dev(n, j))
            cx[g, n] = go(C_X + g * 2 + n, part, part, dev(core=oc))

    half = pl.ds(pl.multiple_of(256 * c, 256), 256)
    for slot, dx in ((1, 3), (2, 1), (3, 2)):
        xq[slot] = go(X_Q + slot - 1, wgt.at[half, pl.ds(0, 512)], wq.at[slot, half], dev(dx=dx))

    def arrived(n, j):
        return strip(lax.rem(place[n] + 4 - j, 4))

    def side_arrivals(g):
        for j in (1, 3, 2):
            for n in (0, 1):
                sw[g, n, j].wait_recv()
                part = kv_w[n].at[groups[g], arrived(n, j)]
                cs[g, n, j] = go(C_SIDE + g * 6 + n * 3 + j - 1, part, part, dev(core=oc))

    acc[2] = dot(tk(0), wq[0])
    side_arrivals(0)
    side_arrivals(1)
    for n in (0, 1):
        cx[0, n].wait_recv()
        for j in (1, 3, 2):
            cs[0, n, j].wait_recv()
        acc[n] += dot(tk(1), kv_w[n][1]) + dot(tk(2), kv_w[n][2])
    for n in (0, 1):
        cx[1, n].wait_recv()
        for j in (1, 3, 2):
            cs[1, n, j].wait_recv()
        r = acc[n] + dot(tk(3), kv_w[n][3])
        for h in range(HEADS):
            proj[4 + 4 * n + h] = r[:, 128 * h:128 * h + 128].astype(BF).reshape(8, 64, HD)

    def rows(j, b):
        return proj[j, pl.ds(2 * b, 2)].reshape(128, HD)

    def span(j, n, m):
        return proj[j, n // 64:m // 64].reshape(m - n, HD)

    fb = [lax.rem(foff[h], 4) for h in range(HEADS)]
    nbk = [noff[h] for h in range(HEADS)]
    for h in range(HEADS):
        for d in (0, 1):
            fkvs[d, h, 0] = proj[4 + h, 2 * fb[h] + d]
            fkvs[d, h, 1] = proj[8 + h, 2 * fb[h] + d]
    me = 2 * y + c
    fin = []
    for j in (0, 1, 2, 3):
        t = lax.rem(y + j, 4)
        for core in (c, oc):
            if j or core is oc:
                fin.append(go(F_KV + len(fin), fkvs.at[core, t], fkvc.at[me], dev(dy=j, core=core)))
    fkvc[me] = fkvs[c, y]
    for h in range(HEADS):
        nks[h, 0] = rows(4 + h, nbk[h])
        nks[h, 1] = rows(8 + h, nbk[h])
    nin = []
    for j in (1, 3, 2):
        t = lax.rem(y + j, 4)
        nin.append(go(N_KV + j - 1, nks.at[t], nkv.at[c, :, y], dev(dy=j)))
    nkv[c, 0, y] = nks[y, 0]
    nkv[c, 1, y] = nks[y, 1]

    cq = {}
    for slot in (1, 2, 3):
        xq[slot].wait_recv()
        cq[slot] = go(C_Q + slot - 1, wq.at[slot, half], wq.at[slot, half], dev(core=oc))

    for cp in fin:
        cp.wait_recv()
    holder = lax.div(foff[y], 4)
    kvf[0] = fkvc[holder]
    ups, dns, maybe = {}, {}, []

    def start_if(cp, needed):
        maybe.append((cp, needed))

        @pl.when(needed)
        def _():
            cp.start()

    def send_up(d, hops):
        ups[d] = rc(R_UP + d - 1, kvf.at[d - hops], kvf.at[d], dev(dz=hops))
        start_if(ups[d], (z + hops < NZ) & (z + hops >= d))

    def wanted_dn(place_z, d):
        late = place_z + d >= NZ
        return late if d % 2 else late | (place_z + d <= 6)

    def send_dn(d, hops):
        src = 0 if d == hops else 16 - d + hops
        dns[d] = rc(R_DN + d - 1, kvf.at[src], kvf.at[16 - d], dev(dz=NZ - hops))
        start_if(dns[d], wanted_dn(lax.rem(z + NZ - hops, NZ), d))

    def got_up(d):
        @pl.when(z >= d)
        def _():
            ups[d].wait_recv()

    def got_dn(d):
        @pl.when(wanted_dn(z, d))
        def _():
            dns[d].wait_recv()

    def ring(d):
        if d:
            got_up(d)
        send_up(d + 2, 2)
        if d:
            got_dn(d)
        if d < 6:
            send_dn(d + 2, 2)
        send_up(d + 1, 1)
        send_dn(d + 1, 1)

    ring(0)
    for cp in nin:
        cp.wait_recv()
    nsib = go(N_SIB, nkv.at[c], nkv.at[c], dev(core=oc))
    odd = lax.rem(z, 2) == 1
    upper = jnp.logical_not(odd) & (z > 0)
    lower = odd & (z < NZ - 1)

    for slot in (1, 2, 3):
        cq[slot].wait_recv()
    r = acc[2] + dot(tk(1), wq[1]) + dot(tk(2), wq[2]) + dot(tk(3), wq[3])
    for h in range(HEADS):
        proj[h] = r[:, 128 * h:128 * h + 128].astype(BF).reshape(8, 64, HD)
    ring(2)
    for h in range(HEADS):
        fqs[h] = rows(h, fb[h])
        nqs[h] = rows(h, nbk[h])
    down = [rc(N_QD + j, nqs.at[lax.rem(y + j, 4)], ncq.at[y], dev(dy=j, dz=NZ - 1)) for j in (0, 1, 2, 3)]

    @pl.when(upper)
    def _():
        for j in (0, 1, 3, 2):
            down[j].start()

    qin = []
    for j in (1, 3, 2):
        t = lax.rem(y + j, 4)
        qin.append(go(N_Q + j - 1, nqs.at[t], nq.at[y], dev(dy=j)))
    nq[y] = nqs[y]
    fqin = []
    for j in (0, 1, 2, 3):
        t = lax.rem(y + j, 4)
        for core in (c, oc):
            if j or core is oc:
                fqin.append(go(F_Q + len(fqin), fqs.at[t], fqc.at[me], dev(dy=j, core=core)))
    fqc[me] = fqs[y]

    def pack(lse):
        t = lse.T[0:16]
        a = t.astype(BF).astype(F32)
        b = (t - a).astype(BF).astype(F32)
        row = lax.broadcasted_iota(jnp.int32, (16, 128), 0)
        return jnp.where(row == 0, a, jnp.where(row == 1, b, t - a - b)).astype(BF)

    qi = lax.broadcasted_iota(jnp.int32, (128, 128), 0)
    ki = lax.broadcasted_iota(jnp.int32, (128, 128), 1)
    causal = ki <= qi

    def local(h, i):
        n = 128 * i
        q = span(h, n, n + 128)
        s1 = jnp.where(causal, qk(q, span(4 + h, n, n + 128)), NEG)
        top = jnp.max(s1, axis=1, keepdims=True)
        if i:
            s0 = qk(q, span(4 + h, 0, n))
            top = jnp.maximum(top, jnp.max(s0, axis=1, keepdims=True))
        p1 = jnp.exp(s1 - top)
        tot = jnp.sum(p1, axis=1, keepdims=True)
        o = pv(p1, span(8 + h, n, n + 128))
        if i:
            p0 = jnp.exp(s0 - top)
            tot = tot + jnp.sum(p0, axis=1, keepdims=True)
            o = o + pv(p0, span(8 + h, 0, n))
        lo[h, i] = o / tot
        ll[h, i] = lanes(top + jnp.log(tot))

    for h in (0, 1):
        for i in range(4):
            local(h, i)
    ring(4)

    def finish(to, i, pairs, tops):
        top = tops[0]
        for t in tops[1:]:
            top = jnp.maximum(top, t)
        tot, o = 0.0, 0.0
        for sc, v in pairs:
            p = jnp.exp(sc - top)
            tot = tot + jnp.sum(p, axis=1, keepdims=True)
            o = o + pv(p, v)
        to[i, 0:128] = (o / tot).astype(BF)
        to[i, 128:144] = pack(lanes(top + jnp.log(tot)))

    def near_plane(i):
        q = nq[i]
        m = 128 * (i + 1)
        sa = qk(q, nkv[c, 0, 0:i + 1].reshape(m, HD))
        sb = qk(q, nkv[oc, 0, 0:i + 1].reshape(m, HD))
        kk = lax.broadcasted_iota(jnp.int32, (128, m), 1)
        qq = lax.broadcasted_iota(jnp.int32, (128, m), 0) + 128 * i
        sa = jnp.where(kk <= qq, sa, NEG)
        sb = jnp.where(kk < 128 * (i + c), sb, NEG)
        finish(nos, i, [(sa, nkv[c, 1, 0:i + 1].reshape(m, HD)), (sb, nkv[oc, 1, 0:i + 1].reshape(m, HD))],
               [jnp.max(sa, axis=1, keepdims=True), jnp.max(sb, axis=1, keepdims=True)])

    nsib.wait_recv()
    for cp in qin:
        cp.wait_recv()
    for i in range(4):
        near_plane(i)
    nback = []
    for j in (1, 3, 2):
        nback.append(go(N_O + j - 1, nos.at[lax.rem(y + j, 4)], nor.at[y], dev(dy=j)))
    nor[y] = nos[y]

    back = [rc(N_OC + j, cos.at[lax.rem(y + j, 4)], cor.at[y], dev(dy=j, dz=1)) for j in (0, 1, 2, 3)]

    @pl.when(lower)
    def _():
        for j in (0, 1, 3, 2):
            down[j].wait_recv()
        for i in range(4):
            q = ncq[i]
            ss = [qk(q, nkv[d, 0].reshape(512, HD)) for d in (0, 1)]
            finish(cos, i, [(ss[d], nkv[d, 1].reshape(512, HD)) for d in (0, 1)],
                   [jnp.max(t, axis=1, keepdims=True) for t in ss])
        for j in (0, 1, 3, 2):
            back[j].start()

    @pl.when(jnp.logical_not(upper))
    def _():
        for h in range(HEADS):
            cor[h, 0:128] = jnp.zeros((128, HD), BF)
            cor[h, 128:144] = jnp.full((16, HD), NEG, BF)

    ring(6)
    for h in (2, 3):
        for i in range(4):
            local(h, i)
    for cp in fqin:
        cp.wait_recv()
    for d in (1, 3, 5):
        got_up(d)
        got_dn(d)

    fq = fqc[holder]
    ranges = ((0, 7), (10, 16), (7, 10))

    def far_scores(a, b):
        m = 64 * (b - a)
        kk = lax.broadcasted_iota(jnp.int32, (128, m), 1) + 64 * a
        qq = lax.broadcasted_iota(jnp.int32, (128, m), 0)
        seen = lax.shift_right_logical(kk, 6) <= z
        if a == 0:
            seen = seen & ((kk >= 64) | (kk + 64 * c <= qq))
        return jnp.where(seen, qk(fq, kvf[a:b, 0].reshape(m, HD)), NEG)

    def far_part(top, a, b, sc):
        p = jnp.exp(sc - top)
        return jnp.sum(p, axis=1, keepdims=True), pv(p, kvf[a:b, 1].reshape(64 * (b - a), HD))

    early = [far_scores(a, b) for a, b in ranges[:2]]
    top0 = jnp.maximum(jnp.max(early[0], axis=1, keepdims=True), jnp.max(early[1], axis=1, keepdims=True))
    parts = [far_part(top0, a, b, sc) for (a, b), sc in zip(ranges[:2], early)]
    got_up(7)
    got_dn(7)
    got_up(8)
    late = far_scores(*ranges[2])
    top = jnp.maximum(top0, jnp.max(late, axis=1, keepdims=True))
    w = jnp.exp(top0 - top)
    tl, ol = far_part(top, *ranges[2], late)
    tot = w * (parts[0][0] + parts[1][0]) + tl
    fos[0:128] = ((w * (parts[0][1] + parts[1][1]) + ol) / tot).astype(BF)
    fos[128:144] = pack(lanes(top + jnp.log(tot)))
    fback = [[], [], [], []]
    n = 0
    for dy in (2, 1, 3, 0):
        for core in (c, oc):
            if dy == 0 and core is c:
                continue
            fback[dy].append(go(F_O + n, fos, fo.at[y, c], dev(dy=dy, core=core)))
            n += 1
    fo[y, c] = fos[...]

    def spread(tile):
        t = tile.astype(F32)
        return jnp.broadcast_to(t[0:1] + t[1:2] + t[2:3], (128, 128)).T

    for cp in nback:
        cp.wait_recv()

    @pl.when(upper)
    def _():
        for j in (0, 1, 3, 2):
            back[j].wait_recv()

    for h in range(HEADS):
        plane_l = spread(nor[h, 128:144])
        cross_l = spread(cor[h, 128:144])
        near_l = jnp.maximum(plane_l, cross_l)
        wp = jnp.exp(plane_l - near_l)
        wc = jnp.exp(cross_l - near_l)
        near_o = wp * nor[h, 0:128].astype(F32) + wc * cor[h, 0:128].astype(F32)
        near_w = wp + wc
        near_at = jnp.full((128, 128), nbk[h], jnp.int32)
        for b in range(4):
            ln = jnp.where(near_at == b, near_l, NEG)
            l0 = ll[h, b]
            best = jnp.maximum(l0, ln)
            w0 = jnp.exp(l0 - best)
            wn = jnp.exp(ln - best)
            lo[h, b] = w0 * lo[h, b] + wn * near_o
            nw[h, b] = w0 + wn * near_w
            ll[h, b] = best
    for dy in (0, 1, 3, 2):
        for cp in fback[dy]:
            cp.wait_recv()
        h = lax.rem(y + 4 - dy, 4)
        far_l = [spread(fo[h, d, 128:144]) for d in (0, 1)]
        far_o = [fo[h, d, 0:128].astype(F32) for d in (0, 1)]
        far_at = jnp.full((128, 128), foff[h], jnp.int32)
        for b in range(4):
            is_far = far_at == lax.rem(seq, 8) * 4 + b
            lf = [jnp.where(is_far, v, NEG) for v in far_l]
            l0 = ll[h, b]
            best = jnp.maximum(l0, jnp.maximum(lf[0], lf[1]))
            w0 = jnp.exp(l0 - best)
            wf = [jnp.exp(v - best) for v in lf]
            num = w0 * lo[h, b] + wf[0] * far_o[0] + wf[1] * far_o[1]
            out[b * 128:b * 128 + 128, pl.ds(pl.multiple_of(h * 128, 128), 128)] = (
                num / (w0 * nw[h, b] + wf[0] + wf[1])).astype(BF)

    for cp in pend:
        cp.wait_send()
    for cp, needed in maybe:
        pl.when(needed)(cp.wait_send)

    @pl.when(upper)
    def _():
        for cp in down:
            cp.wait_send()

    @pl.when(lower)
    def _():
        for cp in back:
            cp.wait_send()


def body(tokens, qkv_weight, near_offset, far_offset):
    vm = pltpu.VMEM
    mixed = pl.pallas_call(
        kernel,
        out_shape=jax.ShapeDtypeStruct((512, 512), BF),
        in_specs=[pl.BlockSpec(memory_space=pl.ANY)] * 4,
        out_specs=pl.BlockSpec(memory_space=pltpu.VMEM),
        scratch_shapes=[
            vm((4, 512, 512), BF),
            vm((4, 512, 512), BF),
            vm((4, 512, 512), BF),
            vm((4, 512, 512), BF),
            vm((3, 512, 512), F32),
            vm((12, 8, 64, 128), BF),
            vm((2, 4, 2, 64, 128), BF),
            vm((4, 128, 128), BF),
            vm((8, 2, 64, 128), BF),
            vm((8, 128, 128), BF),
            vm((16, 2, 64, 128), BF),
            vm((4, 128, 128), BF),
            vm((4, 2, 128, 128), BF),
            vm((4, 128, 128), BF),
            vm((2, 2, 4, 128, 128), BF),
            vm((4, 128, 128), BF),
            vm((4, 144, 128), BF),
            vm((4, 144, 128), BF),
            vm((4, 144, 128), BF),
            vm((4, 144, 128), BF),
            vm((144, 128), BF),
            vm((4, 2, 144, 128), BF),
            vm((4, 4, 128, 128), F32),
            vm((4, 4, 128, 128), F32),
            vm((4, 4, 128, 128), F32),
            pltpu.SMEM((4,), jnp.int32),
            pltpu.SMEM((4,), jnp.int32),
            pltpu.SemaphoreType.DMA((N_SEM,)),
            pltpu.SemaphoreType.DMA((N_SEM,)),
            pltpu.SemaphoreType.DMA((9,)),
        ],
        compiler_params=pltpu.CompilerParams(
            collective_id=0, has_side_effects=True, vmem_limit_bytes=52 * 1024 * 1024),
    )(tokens[0], qkv_weight, near_offset, far_offset)
    return mixed[None]


def solution(mesh):
    in_specs = (P("fsdp", "seq", None), P("fsdp", None), P(), P())
    out_specs = P("fsdp", "seq", None)
    return jax.shard_map(body, mesh=mesh, in_specs=in_specs, out_specs=out_specs, check_vma=False)
```
